32 devices in a mesh: row: 4 (over z), col: 8 (over y, x, core).
Axes of the slice: x: 2, y: 2, z: 4, core: 2. Of those that a mesh axis runs over, the one named last changes fastest.
Arguments:
- row_bases: float32 [4, 128, 4096], P('row', 'col'), may hold values from -4 to 4, as said below
- col_bases: float32 [8, 64, 4096], P('col', 'row'), may hold values from -4 to 4, as said below
- row_transfer: float32 [4, 256, 4096], P('row', 'col'), may hold values from -1 to 1, as said below
- col_transfer: float32 [8, 128, 4096], P('col', 'row'), may hold values from -1 to 1, as said below
- row_order: int32 [4, 8, 16], P('row', 'col'), may hold values from 0 to 15, each once within a row
- col_order: int32 [8, 4, 16], P('col', 'row'), may hold values from 0 to 15, each once within a row
- leaf_pattern: int32 [4, 16, 64], P('row', 'col'), may hold values from 0 to 15
- leaf_blocks: bfloat16 [4, 512, 4096], P('row', 'col'), may hold values from -6 to 6
- root_rows: int32 [4, 8, 32], P('row', 'col'), may hold values from 0 to 7
- root_cols: int32 [4, 8, 32], P('row', 'col'), may hold values from 0 to 3
- root_blocks: bfloat16 [4, 256, 4096], P('row', 'col'), may hold values from -6 to 6
Outputs:
- leaf_coupled: float32 [4, 512, 4096], P('row', 'col')
- root_coupled: float32 [4, 256, 4096], P('row', 'col')
- row_upper_r: float32 [4, 8, 4096], P('row', 'col')
- col_upper_r: float32 [8, 4, 4096], P('col', 'row')
The draws below stay inside these ranges and needn't reach their ends.
Inputs may be any that keep to these rules, and one draw needn't show every extreme that they name: `row_bases`: every leaf basis has full column rank and every Gram matrix of both trees is well conditioned. `col_bases`: every leaf basis has full column rank and every Gram matrix of both trees is well conditioned. `row_transfer`: every transfer matrix is invertible. `col_transfer`: every transfer matrix is invertible.
All inputs are finite; a program needn't handle non-finite values.
Results may differ from the reference program's by a relative error of at most 0.0003.
Values sent between devices are 32-bit elements; how exact they have to be, the bound alone decides.
No kernel may reach another device: no remote copies, remote signals or barrier semaphores. Data moves between devices by JAX's collectives and lax.ppermute only.
A program may use at most 64 MiB of HBM per device.

```python
import math
import jax
import jax.numpy as jnp
from jax import lax

LEAF = 64
RANK = 64
LEAF_DEV = 16
LEAF_PAIRS = 64
ROOT_PAIRS = 32
N_ROW = 4
N_COL = 8


def basis_law(key, outer_count, inner_count):
    key_scale = jax.random.fold_in(key, 3)
    key_jitter = jax.random.fold_in(key, 5)
    scales = jnp.exp(jax.random.uniform(key_scale, (outer_count, inner_count, LEAF, 1), minval=math.log(0.5), maxval=math.log(2.0)))
    jitter = jax.random.truncated_normal(key_jitter, -4.0, 4.0, (outer_count, inner_count, LEAF, RANK))
    identity = jnp.eye(LEAF, RANK, dtype=jnp.float32)
    leaf_basis = scales * (identity + 0.25 * jitter / math.sqrt(RANK))
    return leaf_basis.reshape(outer_count, inner_count, LEAF * RANK)


def transfer_law(key, outer_count, inner_count):
    key_jitter = jax.random.fold_in(key, 7)
    jitter = jax.random.truncated_normal(key_jitter, -4.0, 4.0, (outer_count, inner_count, RANK, RANK))
    identity = jnp.eye(RANK, dtype=jnp.float32)
    matrices = 0.7 * (identity + 0.25 * jitter / math.sqrt(RANK))
    return matrices.reshape(outer_count, inner_count, RANK * RANK)


def draw_row_bases(key, part):
    return basis_law(jax.random.fold_in(key, 11), N_ROW, N_COL * LEAF_DEV)


def draw_col_bases(key, part):
    return basis_law(jax.random.fold_in(key, 13), N_COL, N_ROW * LEAF_DEV)


def draw_row_transfer(key, part):
    return transfer_law(jax.random.fold_in(key, 17), N_ROW, N_COL * 2 * LEAF_DEV)


def draw_col_transfer(key, part):
    return transfer_law(jax.random.fold_in(key, 19), N_COL, N_ROW * 2 * LEAF_DEV)


def with_ends(array, own_key, smallest, high):
    spot = [jax.random.randint(jax.random.fold_in(own_key, axis), (), 0, length) for axis, length in enumerate(array.shape)]
    main_axis = array.shape.index(max(array.shape))
    beside = spot[:main_axis] + [(spot[main_axis] + 1) % array.shape[main_axis]] + spot[main_axis + 1:]
    return array.at[tuple(spot)].set(smallest).at[tuple(beside)].set(high)


def steps_of(stream_key, dims, pieces, smallest, largest):
    def one(axis_at, parts):
        heights = jax.random.uniform(jax.random.fold_in(jax.random.fold_in(stream_key, 6), axis_at), (parts,), jnp.float32, smallest / len(pieces), largest / len(pieces))
        return jnp.repeat(jnp.exp(heights), dims[axis_at] // parts).reshape((-1,) + (1,) * (len(dims) - axis_at - 1))

    factor_of = one(*pieces[0])
    for cut in pieces[1:]:
        factor_of = factor_of * one(*cut)
    return factor_of


def normal_values(stream_key, shape, scale, limit, shards=(), kind=jnp.bfloat16):
    values = scale * jax.random.normal(stream_key, shape, jnp.float32)
    if shards:
        values = values * steps_of(stream_key, shape, shards, -0.22, 0.18)
    return jnp.clip(values, -limit, limit).astype(kind)


def setup_inputs(seed: int = 0) -> dict:
    streams_of = jax.random.split(jax.random.key(seed), 12)
    return {
        "row_bases": draw_row_bases(jax.random.fold_in(streams_of[11], 71), 0),
        "col_bases": draw_col_bases(jax.random.fold_in(streams_of[11], 71), 0),
        "row_transfer": draw_row_transfer(jax.random.fold_in(streams_of[11], 71), 0),
        "col_transfer": draw_col_transfer(jax.random.fold_in(streams_of[11], 71), 0),
        "row_order": jax.vmap(lambda own: jax.random.permutation(own, LEAF_DEV))(jax.random.split(streams_of[4], N_ROW * N_COL)).reshape((N_ROW, N_COL, LEAF_DEV)).astype(jnp.int32),
        "col_order": jax.vmap(lambda own: jax.random.permutation(own, LEAF_DEV))(jax.random.split(streams_of[5], N_COL * N_ROW)).reshape((N_COL, N_ROW, LEAF_DEV)).astype(jnp.int32),
        "leaf_pattern": with_ends(jax.random.randint(streams_of[6], (N_ROW, 2 * N_COL, LEAF_PAIRS), 0, LEAF_DEV), jax.random.fold_in(streams_of[6], 1), 0, LEAF_DEV - 1).astype(jnp.int32),
        "leaf_blocks": normal_values(streams_of[7], (N_ROW, N_COL * LEAF_PAIRS, RANK * RANK), 1.0, 6.0, ((0, 4), (1, 8))),
        "root_rows": with_ends(jax.random.randint(streams_of[8], (N_ROW, N_COL, ROOT_PAIRS), 0, N_COL), jax.random.fold_in(streams_of[8], 1), 0, N_COL - 1).astype(jnp.int32),
        "root_cols": with_ends(jax.random.randint(streams_of[9], (N_ROW, N_COL, ROOT_PAIRS), 0, N_ROW), jax.random.fold_in(streams_of[9], 1), 0, N_ROW - 1).astype(jnp.int32),
        "root_blocks": normal_values(streams_of[10], (N_ROW, N_COL * ROOT_PAIRS, RANK * RANK), 1.0, 6.0, ((0, 4), (1, 8))),
    }


def matmul_high(first_matrix, second_matrix):
    return jnp.matmul(first_matrix, second_matrix, precision=lax.Precision.HIGHEST)

def flipped(matrix):
    return jnp.swapaxes(matrix, -1, -2)

def sandwich(gram, transfer):
    return matmul_high(flipped(transfer), matmul_high(gram, transfer))

def upper_factor(gram):
    return flipped(jnp.linalg.cholesky(gram))

def tree_pass(bases, transfer, order):
    block_count = bases.shape[0]
    leaf_basis = bases.reshape(block_count, LEAF_DEV, LEAF, RANK)
    leaf_gram = jnp.einsum('bpla,bplc->bpac', leaf_basis, leaf_basis, precision=lax.Precision.HIGHEST)
    matrices = transfer.reshape(block_count, 2 * LEAF_DEV, RANK, RANK)
    block_index = jnp.arange(block_count, dtype=jnp.int32)[:, None]
    node_gram = leaf_gram[block_index, order]
    node_up = matrices[block_index, order]
    node_count = LEAF_DEV
    offset = LEAF_DEV
    while node_count > 1:
        contribution = sandwich(node_gram, node_up)
        node_gram = contribution[:, 0::2] + contribution[:, 1::2]
        node_count = node_count // 2
        node_up = matrices[:, offset:offset + node_count]
        offset = offset + node_count
    root_gram = node_gram[:, 0]
    inner_up = matrices[:, 2 * LEAF_DEV - 1]
    highest = root_gram
    node_gram = root_gram
    node_up = node_up[:, 0]
    stride = 1
    while stride < block_count:
        contribution = sandwich(node_gram, node_up)
        node_gram = contribution[0::2] + contribution[1::2]
        node_up = inner_up[stride::2 * stride]
        highest = highest.at[stride::2 * stride].set(node_gram)
        stride = stride * 2
    highest = highest.at[0].set(node_gram[0])
    return (upper_factor(leaf_gram), upper_factor(root_gram), upper_factor(highest))

def reference(row_bases, col_bases, row_transfer, col_transfer, row_order, col_order, leaf_pattern, leaf_blocks, root_rows, root_cols, root_blocks):
    total = N_ROW * N_COL
    row_leaf, row_root, row_high = tree_pass(row_bases.reshape(total, LEAF_DEV, LEAF * RANK), row_transfer.reshape(total, 2 * LEAF_DEV, RANK * RANK), row_order.reshape(total, LEAF_DEV))
    col_leaf, col_root, col_high = tree_pass(col_bases.reshape(total, LEAF_DEV, LEAF * RANK), col_transfer.reshape(total, 2 * LEAF_DEV, RANK * RANK), col_order.reshape(total, LEAF_DEV))
    row_leaf = row_leaf.reshape(N_ROW, N_COL, LEAF_DEV, RANK, RANK)
    col_leaf = jnp.swapaxes(col_leaf.reshape(N_COL, N_ROW, LEAF_DEV, RANK, RANK), 0, 1)
    pattern = leaf_pattern.reshape(N_ROW, N_COL, 2, LEAF_PAIRS)
    leaf_squares = leaf_blocks.astype(jnp.float32).reshape(N_ROW, N_COL, LEAF_PAIRS, RANK, RANK)
    column_index = jnp.arange(N_COL, dtype=jnp.int32)[:, None]

    def leaf_row(operands):
        row_factors, col_factors, pattern_row, squares = operands
        left_factor = row_factors[column_index, pattern_row[:, 0]]
        right_factor = col_factors[column_index, pattern_row[:, 1]]
        return matmul_high(matmul_high(left_factor, squares), flipped(right_factor))
    leaf_coupled = lax.map(leaf_row, (row_leaf, col_leaf, pattern, leaf_squares)).reshape(N_ROW, N_COL * LEAF_PAIRS, RANK * RANK)
    row_root = row_root.reshape(N_ROW, N_COL, RANK, RANK)
    col_root = col_root.reshape(N_COL, N_ROW, RANK, RANK)
    root_squares = root_blocks.astype(jnp.float32).reshape(N_ROW, N_COL, ROOT_PAIRS, RANK, RANK)

    def root_row(operands):
        row_factors, rows_here, cols_here, squares = operands
        left_factor = row_factors[rows_here]
        right_factor = col_root[column_index, cols_here]
        return matmul_high(matmul_high(left_factor, squares), flipped(right_factor))
    root_coupled = lax.map(root_row, (row_root, root_rows, root_cols, root_squares)).reshape(N_ROW, N_COL * ROOT_PAIRS, RANK * RANK)
    row_upper_r = row_high.reshape(N_ROW, N_COL, RANK * RANK)
    col_upper_r = col_high.reshape(N_COL, N_ROW, RANK * RANK)
    return (leaf_coupled, root_coupled, row_upper_r, col_upper_r)
```

```python
import functools

import jax
import jax.numpy as jnp
from jax import lax
from jax.experimental import pallas as pl
from jax.experimental.pallas import tpu as pltpu
from jax.sharding import PartitionSpec as P

RANK = 64
WIDE = 2 * RANK
SUB = 8
NB = RANK // SUB
F32 = jnp.float32
BF16 = jnp.bfloat16
VMEM = pl.BlockSpec(memory_space=pltpu.VMEM)
SMEM = pl.BlockSpec(memory_space=pltpu.SMEM)


def split(x):
    high = x.astype(BF16)
    return high, (x - high.astype(F32)).astype(BF16)


def dot(a, b, rhs_dim=0):
    return lax.dot_general(a, b, (((1,), (rhs_dim,)), ((), ())), preferred_element_type=F32)


def dot3(a, b, rhs_dim=0):
    a_high, a_low = split(a)
    b_high, b_low = split(b)
    return dot(a_high, b_high, rhs_dim) + (dot(a_high, b_low, rhs_dim) + dot(a_low, b_high, rhs_dim))


def lane_half(rows):
    return lax.broadcasted_iota(jnp.int32, (rows, WIDE), 1) < RANK


def swapped(x):
    return pltpu.roll(x, RANK, 1)


def beside(left, right):
    return jnp.where(lane_half(left.shape[0]), left, right)


def sandwich_both(gram, transfer):
    t = transfer.T
    x = dot3(t, gram)
    x = jnp.concatenate([x[:RANK], swapped(x[RANK:])], axis=0)[:, :RANK]
    y = dot3(x, transfer)
    return beside(y[:RANK], y[RANK:])


def unpack_both(left_ref, right_ref, out_ref, count):
    for k in range(RANK // 2):
        a = left_ref[0, :, k * WIDE : (k + 1) * WIDE]
        b = right_ref[0, :, k * WIDE : (k + 1) * WIDE]
        out_ref[pl.ds(2 * k, count, stride=RANK), :] = beside(a, swapped(b))
        out_ref[pl.ds(2 * k + 1, count, stride=RANK), :] = beside(swapped(a), b)


def tree_kernel(
    count,
    row_order,
    col_order,
    row_bases,
    col_bases,
    row_transfer,
    col_transfer,
    leaf_gram,
    row_pay,
    col_pay,
    high,
    basis,
    trans,
):
    unpack_both(row_bases, col_bases, basis, count)
    unpack_both(row_transfer, col_transfer, trans, 2 * count)
    for leaf in range(count):
        u = basis[leaf * RANK : (leaf + 1) * RANK, :]
        g = dot3(u.T, u)
        leaf_gram[leaf * RANK : (leaf + 1) * RANK, :] = beside(g[:RANK], g[RANK:])
    nodes = []
    for q in range(count // 2):
        total = None
        for p in (2 * q, 2 * q + 1):
            r = pl.ds(pl.multiple_of(row_order[0, 0, p] * RANK, RANK), RANK)
            c = pl.ds(pl.multiple_of(col_order[0, 0, p] * RANK, RANK), RANK)
            term = sandwich_both(
                beside(leaf_gram[r, :], leaf_gram[c, :]), beside(trans[r, :], trans[c, :])
            )
            total = term if total is None else total + term
        nodes.append(total)
    offset = count
    while len(nodes) > 1:
        terms = []
        for q, gram in enumerate(nodes):
            terms.append(
                sandwich_both(gram, trans[(offset + q) * RANK : (offset + q + 1) * RANK, :])
            )
        offset += len(nodes)
        nodes = [terms[2 * q] + terms[2 * q + 1] for q in range(len(terms) // 2)]
    gram = nodes[0]
    term = sandwich_both(gram, trans[offset * RANK : (offset + 1) * RANK, :])
    first = trans[(offset + 1) * RANK : (offset + 2) * RANK, :]
    high[...] = gram
    row_pay[0:RANK, :] = beside(term, swapped(first))
    row_pay[RANK:WIDE, :] = gram
    col_pay[0:RANK, :] = beside(swapped(term), first)
    col_pay[RANK:WIDE, :] = swapped(gram)


def step_kernel(trees, last, held, extra, flags, own, recv, high_in, *refs):
    refs = list(refs)
    before = refs.pop(0) if extra else None
    pay_out = refs.pop(0) if len(trees) > len(last) or held else None
    high_out = refs.pop(0)
    base = 0
    if extra:
        pay_out[0:RANK, :] = before[0:RANK, :]
        base = RANK
    high = high_in[...]
    for slot, name in enumerate(trees):
        upper = flags[2 * slot] > 0
        take = flags[2 * slot + 1] > 0
        mine = own[slot * RANK : (slot + 1) * RANK, :]
        theirs = recv[slot * RANK : (slot + 1) * RANK, :]
        total = mine + theirs
        picked = beside(total, high) if name == "r" else beside(high, swapped(total))
        high = jnp.where(take, picked, high)
        if name not in last:
            transfer = jnp.where(upper, mine, theirs)
            first = jnp.where(upper, theirs, mine)
            x = dot3(transfer.T[RANK:], total[:, :RANK])
            term = swapped(dot3(x, transfer))
            pay_out[base : base + RANK, :] = beside(term, first)
            base += RANK
    high_out[...] = high
    if extra:
        pay_out[base : base + RANK, :] = before[RANK:WIDE, :]
    elif held:
        upper = flags[0] > 0
        start = len(trees) * RANK
        if held == 1:
            mine = own[start : start + RANK, :]
            theirs = recv[start : start + RANK, :]
            pay_out[base : base + RANK, :] = jnp.where(
                upper, beside(theirs, swapped(mine)), beside(mine, swapped(theirs))
            )
        else:
            rows = held // 2 * RANK
            mine = own[start : start + rows, :]
            theirs = recv[start : start + rows, :]
            pay_out[base : base + rows, :] = jnp.where(upper, theirs, mine)
            pay_out[base + rows : base + 2 * rows, :] = jnp.where(upper, mine, theirs)


def chol_lanes(a_ref, r_ref):
    sub = lax.broadcasted_iota(jnp.int32, (SUB, WIDE), 0)

    def at(q):
        return slice(SUB * q, SUB * (q + 1))

    def spread(i, j):
        return r_ref[i, pl.ds(j, SUB, stride=0), :]

    def less(value, f, row):
        return lax.sub(value, lax.mul(f, row))

    for p in range(NB):
        i0 = SUB * p
        acc = [a_ref[i0 + r, at(p), :] for r in range(SUB)]
        scale = []
        for r in range(SUB):
            inv = lax.rsqrt(jnp.broadcast_to(acc[r][r : r + 1, :], (SUB, WIDE)))
            scale.append(inv)
            row = jnp.where(sub >= r, acc[r] * inv, 0.0)
            r_ref[i0 + r, at(p), :] = row
            for r2 in range(r + 1, SUB):
                acc[r2] = less(acc[r2], jnp.broadcast_to(row[r2 : r2 + 1, :], (SUB, WIDE)), row)
        for q in range(p + 1, NB):
            x = [a_ref[i0 + r, at(q), :] for r in range(SUB)]
            for r in range(SUB):
                x[r] = lax.mul(x[r], scale[r])
                r_ref[i0 + r, at(q), :] = x[r]
                for r2 in range(r + 1, SUB):
                    x[r2] = less(x[r2], spread(i0 + r, i0 + r2), x[r])
        for pi in range(p + 1, NB):
            for q0 in range(pi, NB, 2):
                qs = range(q0, min(q0 + 2, NB))
                acc2 = {(r, q): a_ref[SUB * pi + r, at(q), :] for r in range(SUB) for q in qs}
                for k in range(SUB):
                    rows = {q: r_ref[i0 + k, at(q), :] for q in qs}
                    for r in range(SUB):
                        f = spread(i0 + k, SUB * pi + r)
                        for q in qs:
                            acc2[r, q] = less(acc2[r, q], f, rows[q])
                for (r, q), value in acc2.items():
                    a_ref[SUB * pi + r, at(q), :] = value


def load_lanes(slots_ref, a_ref, count):
    for i in range(RANK):
        b0 = SUB * (i // SUB)
        t = slots_ref[pl.ds(i, count, stride=RANK), :].T
        a_ref[i, b0:RANK, 0 : 2 * count] = jnp.concatenate([t[b0:RANK], t[RANK + b0 :]], axis=1)


def factor_row(r_ref, i, lanes):
    b0 = SUB * (i // SUB)
    t = r_ref[i, b0:RANK, 0:lanes]
    if b0:
        t = jnp.concatenate([jnp.zeros((b0, lanes), F32), t], axis=0)
    return t.T


def chol_table_kernel(count, sources, *refs):
    inputs = refs[: len(sources)]
    table, a_ref, r_ref = refs[len(sources) : len(sources) + 3]
    if len(sources) > 1:
        slots = refs[len(sources) + 3]
        base = 0
        for ref, (start, rows) in zip(inputs, sources):
            slots[base : base + rows, :] = ref[start : start + rows, :]
            base += rows
    else:
        slots = inputs[0]
    load_lanes(slots, a_ref, count)
    chol_lanes(a_ref, r_ref)
    for i in range(RANK):
        table[pl.ds(i, 2 * count, stride=RANK), :] = factor_row(r_ref, i, 2 * count)


def final_kernel(high, row_out, col_out, slots, a_ref, r_ref):
    slots[0:RANK, :] = high[...]
    load_lanes(slots, a_ref, SUB)
    chol_lanes(a_ref, r_ref)
    for k in range(RANK // 2):
        even = factor_row(r_ref, 2 * k, 2 * SUB)
        odd = factor_row(r_ref, 2 * k + 1, 2 * SUB)
        both = jnp.concatenate([even, odd], axis=1)
        row_out[0, 0:1, k * WIDE : (k + 1) * WIDE] = both[0:1]
        col_out[0, 0:1, k * WIDE : (k + 1) * WIDE] = both[SUB : SUB + 1]


def couple_kernel(pairs, left_of, right_of, left_pick, right_pick, table, blocks, out, s_ref, y_ref):
    for k in range(RANK // 2):
        slab = blocks[0, :, k * WIDE : (k + 1) * WIDE].astype(F32)
        s_ref[pl.ds(2 * k, pairs, stride=RANK), :] = slab[:, :RANK]
        s_ref[pl.ds(2 * k + 1, pairs, stride=RANK), :] = swapped(slab)[:, :RANK]

    def one(b, carry):
        t = pl.multiple_of(left_of(left_pick, b) * RANK, RANK)
        s = pl.multiple_of(right_of(right_pick, b) * RANK, RANK)
        at = pl.ds(pl.multiple_of(b * RANK, RANK), RANK)
        left_high, left_low = split(table[pl.ds(t, RANK), :])
        block = s_ref[at, :].astype(BF16)
        x = dot(left_high, block) + dot(left_low, block)
        y_ref[at, :] = dot3(x, table[pl.ds(s, RANK), :], 1)
        return carry

    lax.fori_loop(0, pairs, one, 0, unroll=8)
    for k in range(RANK // 2):
        even = y_ref[pl.ds(2 * k, pairs, stride=RANK), :]
        odd = y_ref[pl.ds(2 * k + 1, pairs, stride=RANK), :]
        out[0, :, k * WIDE : (k + 1) * WIDE] = jnp.concatenate([even, odd], axis=1)


def shape(*dims):
    return jax.ShapeDtypeStruct(dims, F32)


def scratch(rows, lanes=WIDE):
    return pltpu.VMEM((rows, lanes), F32)


def call(kernel, outs, specs, name, scratches=(), flops=0, moved=0):
    return pl.pallas_call(
        kernel,
        out_shape=outs,
        in_specs=specs,
        out_specs=jax.tree.map(lambda _: VMEM, outs),
        scratch_shapes=list(scratches),
        name=name,
        cost_estimate=pl.CostEstimate(flops=flops, bytes_accessed=moved, transcendentals=0),
    )


def partner(value, axis, bit):
    return lax.ppermute(value, axis, [(i, i ^ 1 << bit) for i in range(lax.axis_size(axis))])


def body(
    row_bases,
    col_bases,
    row_transfer,
    col_transfer,
    row_order,
    col_order,
    leaf_pattern,
    leaf_blocks,
    root_rows,
    root_cols,
    root_blocks,
):
    count = row_bases.shape[1]
    leaf_pairs = leaf_blocks.shape[1]
    root_pairs = root_blocks.shape[1]
    nr, nc = lax.axis_size("row"), lax.axis_size("col")
    lr, lc = nr.bit_length() - 1, nc.bit_length() - 1
    i, j = lax.axis_index("row"), lax.axis_index("col")
    place = {"r": i * nc + j, "c": j * nr + i}

    leaf_gram, row_pay, col_pay, high = call(
        functools.partial(tree_kernel, count),
        [shape(count * RANK, WIDE), shape(WIDE, WIDE), shape(WIDE, WIDE), shape(RANK, WIDE)],
        [SMEM, SMEM, VMEM, VMEM, VMEM, VMEM],
        "local_tree",
        [scratch(count * RANK), scratch(2 * count * RANK)],
    )(row_order, col_order, row_bases, col_bases, row_transfer, col_transfer)

    def flags(levels):
        values = []
        for name, level in levels:
            span = 1 << level
            d = place[name]
            take = d % (2 * span) == span
            if level == lr + lc - 1:
                take = take | (d == 0)
            values += [(d // span) % 2, take.astype(jnp.int32)]
        return jnp.stack(values)

    def step(levels, pay, axis, bit, high, held=0, extra=None):
        trees = tuple(name for name, _ in levels)
        last = tuple(name for name, level in levels if level == lr + lc - 1)
        recv = partner(pay, axis, bit)
        rows = (len(trees) - len(last)) * RANK + held * RANK
        if extra is not None:
            rows = (len(trees) - len(last)) * RANK + WIDE
        outs = [shape(RANK, WIDE)]
        if rows:
            outs = [shape(rows, WIDE)] + outs
        args = [flags(levels), pay, recv, high] + ([] if extra is None else [extra])
        result = call(
            functools.partial(step_kernel, trees, last, held, extra is not None),
            outs,
            [SMEM] + [VMEM] * (len(args) - 1),
            "step",
        )(*args)
        return list(result) if rows else [None, *result]

    pay = col_pay
    for h in range(lr):
        pay, high = step([("c", h)], pay, "row", h, high, held=1 << h)
    col_roots = pay
    pay = jnp.concatenate([row_pay[:RANK], pay[:RANK], row_pay[RANK:]], axis=0)
    for h in range(lc):
        pay, high = step([("r", h), ("c", lr + h)], pay, "col", h, high, held=1 << h)
    row_roots = pay
    pay = pay[:RANK]
    for h in range(lr):
        pay, high = step([("r", lc + h)], pay, "row", h, high)

    big = [pltpu.VMEM((RANK, RANK, WIDE), F32)] * 2
    leaf_table = call(
        functools.partial(chol_table_kernel, count, ((0, count * RANK),)),
        shape(2 * count * RANK, RANK),
        [VMEM],
        "leaf_factors",
        big,
    )(leaf_gram)
    leaf_coupled = call(
        functools.partial(
            couple_kernel,
            leaf_pairs,
            lambda ref, b: ref[0, 0, b],
            lambda ref, b: ref[0, 1, b] + count,
        ),
        shape(1, leaf_pairs, RANK * RANK),
        [SMEM, SMEM, VMEM, VMEM],
        "leaf_couple",
        [scratch(leaf_pairs * RANK, RANK), scratch(leaf_pairs * RANK, RANK)],
    )(leaf_pattern, leaf_pattern, leaf_table, leaf_blocks)

    row_slots, col_slots = nc // 2, nr // 2
    slots = -(-(row_slots + col_slots) // SUB) * SUB
    root_table = call(
        functools.partial(
            chol_table_kernel,
            slots,
            ((row_roots.shape[0] - row_slots * RANK, row_slots * RANK), (RANK, col_slots * RANK)),
        ),
        shape(2 * slots * RANK, RANK),
        [VMEM, VMEM],
        "root_factors",
        big + [scratch(slots * RANK)],
    )(row_roots, col_roots)
    root_coupled = call(
        functools.partial(
            couple_kernel,
            root_pairs,
            lambda ref, b: (ref[0, 0, b] & 1) * slots + (ref[0, 0, b] >> 1),
            lambda ref, b: (ref[0, 0, b] & 1) * slots + (ref[0, 0, b] >> 1) + row_slots,
        ),
        shape(1, root_pairs, RANK * RANK),
        [SMEM, SMEM, VMEM, VMEM],
        "root_couple",
        [scratch(root_pairs * RANK, RANK), scratch(root_pairs * RANK, RANK)],
    )(root_rows, root_cols, root_table, root_blocks)

    row_upper_r, col_upper_r = call(
        final_kernel,
        [shape(1, 1, RANK * RANK), shape(1, 1, RANK * RANK)],
        [VMEM],
        "upper_factors",
        [scratch(SUB * RANK)] + big,
    )(high)
    return (leaf_coupled, root_coupled, row_upper_r, col_upper_r)


def solution(mesh):
    return jax.shard_map(
        body,
        mesh=mesh,
        in_specs=(
            P("row", "col", None),
            P("col", "row", None),
            P("row", "col", None),
            P("col", "row", None),
            P("row", "col", None),
            P("col", "row", None),
            P("row", "col", None),
            P("row", "col", None),
            P("row", "col", None),
            P("row", "col", None),
            P("row", "col", None),
        ),
        out_specs=(
            P("row", "col", None),
            P("row", "col", None),
            P("row", "col", None),
            P("col", "row", None),
        ),
        check_vma=False,
    )
```

```python
import functools

import jax
import jax.numpy as jnp
from jax import lax
from jax.experimental import pallas as pl
from jax.experimental.pallas import tpu as pltpu
from jax.sharding import PartitionSpec as P


RANK = 64
WIDE = 2 * RANK
SUB = 8
NB = RANK // SUB
F32 = jnp.float32
BF16 = jnp.bfloat16
VMEM = pl.BlockSpec(memory_space=pltpu.VMEM)
SMEM = pl.BlockSpec(memory_space=pltpu.SMEM)


def split(x):
    high = x.astype(BF16)
    return high, (x - high.astype(F32)).astype(BF16)


def dot(a, b, rhs_dim=0):
    return lax.dot_general(a, b, (((1,), (rhs_dim,)), ((), ())), preferred_element_type=F32)


def dot3(a, b):
    a_high, a_low = split(a)
    b_high, b_low = split(b)
    return dot(a_high, b_high) + (dot(a_high, b_low) + dot(a_low, b_high))


def stacked(x, axis=0):
    return jnp.concatenate(split(x), axis=axis)


def lane_half(rows):
    return lax.broadcasted_iota(jnp.int32, (rows, WIDE), 1) < RANK


def swapped(x):
    return pltpu.roll(x, RANK, 1)


def beside(left, right):
    return jnp.where(lane_half(left.shape[0]), left, right)


def dot_both(a, b):
    y = dot(stacked(a), stacked(b))
    return beside(y[:RANK], y[RANK:WIDE]) + beside(y[WIDE : WIDE + RANK], y[WIDE + RANK :])


def sandwich_both(gram, transfer):
    x = dot(stacked(jnp.concatenate([transfer, transfer], axis=0).T), stacked(gram))
    x = x[:WIDE] + x[WIDE:]
    top, low = x[:RANK], x[RANK:]
    return dot_both(
        jnp.concatenate([beside(top, swapped(top)), beside(swapped(low), low)], axis=0), transfer
    )


def unpack_both(left_ref, right_ref, out_ref, count):
    for k in range(RANK // 2):
        a = left_ref[0, :, k * WIDE : (k + 1) * WIDE]
        b = right_ref[0, :, k * WIDE : (k + 1) * WIDE]
        out_ref[pl.ds(2 * k, count, stride=RANK), :] = beside(a, swapped(b))
        out_ref[pl.ds(2 * k + 1, count, stride=RANK), :] = beside(swapped(a), b)


def tree_kernel(
    count,
    row_order,
    col_order,
    row_bases,
    col_bases,
    row_transfer,
    col_transfer,
    leaf_gram,
    row_pay,
    col_pay,
    high,
    basis,
    trans,
):
    unpack_both(row_bases, col_bases, basis, count)
    unpack_both(row_transfer, col_transfer, trans, 2 * count)
    for leaf in range(count):
        u = basis[leaf * RANK : (leaf + 1) * RANK, :]
        leaf_gram[leaf * RANK : (leaf + 1) * RANK, :] = dot_both(
            jnp.concatenate([u, u], axis=0).T, u
        )
    nodes = []
    for q in range(count // 2):
        total = None
        for p in (2 * q, 2 * q + 1):
            r = pl.ds(pl.multiple_of(row_order[0, 0, p] * RANK, RANK), RANK)
            c = pl.ds(pl.multiple_of(col_order[0, 0, p] * RANK, RANK), RANK)
            term = sandwich_both(
                beside(leaf_gram[r, :], leaf_gram[c, :]), beside(trans[r, :], trans[c, :])
            )
            total = term if total is None else total + term
        nodes.append(total)
    offset = count
    while len(nodes) > 1:
        terms = []
        for q, gram in enumerate(nodes):
            terms.append(
                sandwich_both(gram, trans[(offset + q) * RANK : (offset + q + 1) * RANK, :])
            )
        offset += len(nodes)
        nodes = [terms[2 * q] + terms[2 * q + 1] for q in range(len(terms) // 2)]
    gram = nodes[0]
    term = sandwich_both(gram, trans[offset * RANK : (offset + 1) * RANK, :])
    first = trans[(offset + 1) * RANK : (offset + 2) * RANK, :]
    high[...] = gram
    row_pay[0:RANK, :] = beside(term, swapped(first))
    row_pay[RANK:WIDE, :] = gram
    col_pay[0:RANK, :] = beside(swapped(term), first)
    col_pay[RANK:WIDE, :] = swapped(gram)


def step_kernel(levels, top, sizes, held, apart, extra, own, recv, high_in, *refs):
    refs = list(refs)
    before = refs.pop(0) if extra else None
    high_out = refs.pop(0)
    roots_out = refs.pop() if apart else None
    pay_out = refs.pop(0) if refs else None
    nr, nc = sizes
    i, j = lax.axis_index("row"), lax.axis_index("col")
    base = 0
    if extra:
        pay_out[0:RANK, :] = before[0:RANK, :]
        base = RANK
    high = high_in[...]
    uppers = []
    for slot, (name, level) in enumerate(levels):
        d = i * nc + j if name == "r" else j * nr + i
        span = 1 << level
        upper = lax.rem(lax.div(d, span), 2) == 1
        uppers.append(upper)
        take = lax.rem(d, 2 * span) == span
        if level == top:
            take = jnp.logical_or(take, d == 0)
        mine = own[slot * RANK : (slot + 1) * RANK, :]
        theirs = recv[slot * RANK : (slot + 1) * RANK, :]
        total = mine + theirs
        if level < top:
            transfer = jnp.where(upper, mine, theirs)
            first = jnp.where(upper, theirs, mine)
            x = dot3(transfer.T[RANK:], total[:, :RANK])
            pay_out[base : base + RANK, :] = beside(swapped(dot3(x, transfer)), first)
            base += RANK
        picked = beside(total, high) if name == "r" else beside(high, swapped(total))
        high = jnp.where(take, picked, high)
    high_out[...] = high
    if extra:
        pay_out[base : base + RANK, :] = before[RANK:WIDE, :]
    if held:
        upper = uppers[0]
        start = len(levels) * RANK
        if roots_out is None:
            roots_out = pay_out.at[base:, :]
        if held == 1:
            mine = own[start : start + RANK, :]
            theirs = recv[start : start + RANK, :]
            roots_out[0:RANK, :] = jnp.where(
                upper, beside(theirs, swapped(mine)), beside(mine, swapped(theirs))
            )
        else:
            rows = held // 2 * RANK
            mine = own[start : start + rows, :]
            theirs = recv[start : start + rows, :]
            roots_out[0:rows, :] = jnp.where(upper, theirs, mine)
            roots_out[rows : 2 * rows, :] = jnp.where(upper, mine, theirs)


def chol_lanes(a_ref, r_ref):
    sub = lax.broadcasted_iota(jnp.int32, (SUB, WIDE), 0)

    def at(q):
        return slice(SUB * q, SUB * (q + 1))

    def spread(i, j):
        return r_ref[i, pl.ds(j, SUB, stride=0), :]

    def less(value, f, row):
        return lax.sub(value, lax.mul(f, row))

    for p in range(NB):
        i0 = SUB * p
        acc = [a_ref[i0 + r, at(p), :] for r in range(SUB)]
        scale = []
        for r in range(SUB):
            inv = lax.rsqrt(jnp.broadcast_to(acc[r][r : r + 1, :], (SUB, WIDE)))
            scale.append(inv)
            row = jnp.where(sub >= r, acc[r] * inv, 0.0)
            r_ref[i0 + r, at(p), :] = row
            for r2 in range(r + 1, SUB):
                acc[r2] = less(acc[r2], jnp.broadcast_to(row[r2 : r2 + 1, :], (SUB, WIDE)), row)
        for q in range(p + 1, NB):
            x = [a_ref[i0 + r, at(q), :] for r in range(SUB)]
            for r in range(SUB):
                x[r] = lax.mul(x[r], scale[r])
                r_ref[i0 + r, at(q), :] = x[r]
                for r2 in range(r + 1, SUB):
                    x[r2] = less(x[r2], spread(i0 + r, i0 + r2), x[r])
        for pi in range(p + 1, NB):
            for q0 in range(pi, NB, 2):
                qs = range(q0, min(q0 + 2, NB))
                acc2 = {(r, q): a_ref[SUB * pi + r, at(q), :] for r in range(SUB) for q in qs}
                for k in range(SUB):
                    rows = {q: r_ref[i0 + k, at(q), :] for q in qs}
                    for r in range(SUB):
                        f = spread(i0 + k, SUB * pi + r)
                        for q in qs:
                            acc2[r, q] = less(acc2[r, q], f, rows[q])
                for (r, q), value in acc2.items():
                    a_ref[SUB * pi + r, at(q), :] = value


def load_lanes(slots_ref, a_ref, count):
    for i in range(RANK):
        b0 = SUB * (i // SUB)
        t = slots_ref[pl.ds(i, count, stride=RANK), :].T
        a_ref[i, b0:RANK, 0 : 2 * count] = jnp.concatenate([t[b0:RANK], t[RANK + b0 :]], axis=1)


def factor_row(r_ref, i, lanes):
    b0 = SUB * (i // SUB)
    t = r_ref[i, b0:RANK, 0:lanes]
    if b0:
        t = jnp.concatenate([jnp.zeros((b0, lanes), F32), t], axis=0)
    return t.T


def chol_table_kernel(count, sources, *refs):
    inputs = refs[: len(sources)]
    table, a_ref, r_ref, factor = refs[len(sources) : len(sources) + 4]
    if len(sources) > 1:
        slots = refs[len(sources) + 4]
        base = 0
        for ref in inputs:
            slots[base : base + ref.shape[0], :] = ref[...]
            base += ref.shape[0]
    else:
        slots = inputs[0]
    load_lanes(slots, a_ref, count)
    chol_lanes(a_ref, r_ref)
    for i in range(RANK):
        factor[pl.ds(i, 2 * count, stride=RANK), :] = factor_row(r_ref, i, 2 * count)
    for b in range(2 * count):
        table[b * WIDE : (b + 1) * WIDE, :] = stacked(factor[b * RANK : (b + 1) * RANK, :])


def final_kernel(high, row_out, col_out, slots, a_ref, r_ref):
    slots[0:RANK, :] = high[...]
    load_lanes(slots, a_ref, SUB)
    chol_lanes(a_ref, r_ref)
    for k in range(RANK // 2):
        even = factor_row(r_ref, 2 * k, 2 * SUB)
        odd = factor_row(r_ref, 2 * k + 1, 2 * SUB)
        both = jnp.concatenate([even, odd], axis=1)
        row_out[0, 0:1, k * WIDE : (k + 1) * WIDE] = both[0:1]
        col_out[0, 0:1, k * WIDE : (k + 1) * WIDE] = both[SUB : SUB + 1]


def couple_kernel(start, pairs, left_of, right_of, left_pick, right_pick, table, blocks, y_ref, s_ref):
    for k in range(RANK // 2):
        slab = blocks[0, start : start + pairs, k * WIDE : (k + 1) * WIDE].astype(F32)
        s_ref[pl.ds(2 * k, pairs, stride=RANK), :] = slab[:, :RANK]
        s_ref[pl.ds(2 * k + 1, pairs, stride=RANK), :] = swapped(slab)[:, :RANK]

    def one(b, carry):
        t = pl.multiple_of(left_of(left_pick, start + b) * WIDE, WIDE)
        s = pl.multiple_of(right_of(right_pick, start + b) * WIDE, WIDE)
        at = pl.ds(pl.multiple_of(b * RANK, RANK), RANK)
        x = dot(table[pl.ds(t, WIDE), :], s_ref[at, :].astype(BF16))
        y = dot(stacked(x[:RANK] + x[RANK:]), table[pl.ds(s, WIDE), :], 1)
        y = y[:RANK] + y[RANK:]
        y_ref[at, :] = y + swapped(y)
        return carry

    lax.fori_loop(0, pairs, one, 0, unroll=8)


def pack_kernel(sizes, *refs):
    inputs, out = refs[: len(sizes)], refs[len(sizes)]
    for k in range(RANK // 2):
        base = 0
        for pairs, y_ref in zip(sizes, inputs):
            out[0, base : base + pairs, k * WIDE : (k + 1) * WIDE] = beside(
                y_ref[pl.ds(2 * k, pairs, stride=RANK), :],
                y_ref[pl.ds(2 * k + 1, pairs, stride=RANK), :],
            )
            base += pairs


def shape(*dims):
    return jax.ShapeDtypeStruct(dims, F32)


def scratch(rows, lanes=WIDE):
    return pltpu.VMEM((rows, lanes), F32)


def call(kernel, outs, specs, scratches=(), limit=8):
    return pl.pallas_call(
        kernel,
        out_shape=outs,
        in_specs=specs,
        out_specs=jax.tree.map(lambda _: VMEM, outs),
        scratch_shapes=list(scratches),
        compiler_params=pltpu.CompilerParams(vmem_limit_bytes=limit << 20),
    )


def partner(value, axis, bit):
    return lax.ppermute(value, axis, [(i, i ^ 1 << bit) for i in range(lax.axis_size(axis))])


def body(
    row_bases,
    col_bases,
    row_transfer,
    col_transfer,
    row_order,
    col_order,
    leaf_pattern,
    leaf_blocks,
    root_rows,
    root_cols,
    root_blocks,
):
    count = row_bases.shape[1]
    leaf_pairs = leaf_blocks.shape[1]
    root_pairs = root_blocks.shape[1]
    nr, nc = lax.axis_size("row"), lax.axis_size("col")
    lr, lc = nr.bit_length() - 1, nc.bit_length() - 1
    top = lr + lc - 1

    leaf_gram, row_pay, col_pay, high = call(
        functools.partial(tree_kernel, count),
        [shape(count * RANK, WIDE), shape(WIDE, WIDE), shape(WIDE, WIDE), shape(RANK, WIDE)],
        [SMEM, SMEM, VMEM, VMEM, VMEM, VMEM],
        [scratch(count * RANK), scratch(2 * count * RANK)],
    )(row_order, col_order, row_bases, col_bases, row_transfer, col_transfer)

    def step(levels, pay, axis, bit, high, held=0, apart=False, extra=None):
        recv = partner(pay, axis, bit)
        rows = sum(level < top for _, level in levels) * RANK
        rows += 0 if apart else held * RANK
        rows += 0 if extra is None else WIDE
        outs = [shape(RANK, WIDE)]
        if rows:
            outs.append(shape(rows, WIDE))
        if apart:
            outs.append(shape(held * RANK, WIDE))
        args = [pay, recv, high] + ([] if extra is None else [extra])
        result = call(
            functools.partial(step_kernel, levels, top, (nr, nc), held, apart, extra is not None),
            outs,
            [VMEM] * len(args),
            limit=2 + held // 4,
        )(*args)
        return result

    pay = col_pay
    for h in range(lr):
        done = h == lr - 1
        high, pay, *rest = step(
            [("c", h)],
            pay,
            "row",
            h,
            high,
            held=1 << h,
            apart=done,
            extra=row_pay if done else None,
        )
    col_roots = rest[0]
    for h in range(lc):
        done = h == lc - 1
        high, pay, *rest = step(
            [("r", h), ("c", lr + h)], pay, "col", h, high, held=1 << h, apart=done
        )
    row_roots = rest[0]
    for h in range(lr):
        high, *rest = step([("r", lc + h)], pay, "row", h, high)
        pay = rest[0] if rest else None

    big = [pltpu.VMEM((RANK, RANK, WIDE), F32)] * 2

    def table(count, *sources):
        return call(
            functools.partial(chol_table_kernel, count, [x.shape for x in sources]),
            jax.ShapeDtypeStruct((2 * count * WIDE, RANK), BF16),
            [VMEM] * len(sources),
            big
            + [scratch(2 * count * RANK, RANK)]
            + ([scratch(count * RANK)] if len(sources) > 1 else []),
            limit=5 + count // 3,
        )(*sources)

    def couple(parts, total, left_of, right_of, left_pick, right_pick, table, blocks):
        pieces, start = [], 0
        for pairs in parts:
            pieces.append(
                call(
                    functools.partial(couple_kernel, start, pairs, left_of, right_of),
                    shape(pairs * RANK, WIDE),
                    [SMEM, SMEM, VMEM, VMEM],
                    [scratch(pairs * RANK, RANK)],
                )(left_pick, right_pick, table, blocks)
            )
            start += pairs
        return call(
            functools.partial(pack_kernel, parts), shape(1, total, RANK * RANK), [VMEM] * len(parts)
        )(*pieces)

    quarter = leaf_pairs // 4
    leaf_coupled = couple(
        (quarter, quarter, 2 * quarter),
        leaf_pairs,
        lambda ref, b: ref[0, 0, b],
        lambda ref, b: ref[0, 1, b] + count,
        leaf_pattern,
        leaf_pattern,
        table(count, leaf_gram),
        leaf_blocks,
    )
    row_slots, col_slots = nc // 2, nr // 2
    slots = -(-(row_slots + col_slots) // SUB) * SUB
    root_coupled = couple(
        (root_pairs,),
        root_pairs,
        lambda ref, b: (ref[0, 0, b] & 1) * slots + (ref[0, 0, b] >> 1),
        lambda ref, b: (ref[0, 0, b] & 1) * slots + (ref[0, 0, b] >> 1) + row_slots,
        root_rows,
        root_cols,
        table(slots, row_roots, col_roots),
        root_blocks,
    )
    row_upper_r, col_upper_r = call(
        final_kernel,
        [shape(1, 1, RANK * RANK), shape(1, 1, RANK * RANK)],
        [VMEM],
        [scratch(SUB * RANK)] + big,
    )(high)
    return (leaf_coupled, root_coupled, row_upper_r, col_upper_r)


def solution(mesh):
    return jax.shard_map(
        body,
        mesh=mesh,
        in_specs=(
            P("row", "col", None),
            P("col", "row", None),
            P("row", "col", None),
            P("col", "row", None),
            P("row", "col", None),
            P("col", "row", None),
            P("row", "col", None),
            P("row", "col", None),
            P("row", "col", None),
            P("row", "col", None),
            P("row", "col", None),
        ),
        out_specs=(
            P("row", "col", None),
            P("row", "col", None),
            P("row", "col", None),
            P("col", "row", None),
        ),
        check_vma=False,
    )
```

```python
import functools

import jax
import jax.numpy as jnp
from jax import lax
from jax.experimental import pallas as pl
from jax.experimental.pallas import tpu as pltpu
from jax.sharding import PartitionSpec as P


RANK = 64
WIDE = 2 * RANK
SUB = 8
NB = RANK // SUB
F32 = jnp.float32
BF16 = jnp.bfloat16
VMEM = pl.BlockSpec(memory_space=pltpu.VMEM)
SMEM = pl.BlockSpec(memory_space=pltpu.SMEM)


def split(x):
    high = x.astype(BF16)
    return high, (x - high.astype(F32)).astype(BF16)


def dot(a, b, rhs_dim=0):
    return lax.dot_general(a, b, (((1,), (rhs_dim,)), ((), ())), preferred_element_type=F32)


def dot3(a, b):
    a_high, a_low = split(a)
    b_high, b_low = split(b)
    return dot(a_high, b_high) + (dot(a_high, b_low) + dot(a_low, b_high))


def stacked(x, axis=0):
    return jnp.concatenate(split(x), axis=axis)


def lane_half(rows):
    return lax.broadcasted_iota(jnp.int32, (rows, WIDE), 1) < RANK


def swapped(x):
    return pltpu.roll(x, RANK, 1)


def beside(left, right):
    return jnp.where(lane_half(left.shape[0]), left, right)


def dot_both(a, b):
    y = dot(stacked(a), stacked(b))
    return beside(y[:RANK], y[RANK:WIDE]) + beside(y[WIDE : WIDE + RANK], y[WIDE + RANK :])


def sandwich_both(gram, transfer):
    x = dot(stacked(jnp.concatenate([transfer, transfer], axis=0).T), stacked(gram))
    x = x[:WIDE] + x[WIDE:]
    top, low = x[:RANK], x[RANK:]
    return dot_both(
        jnp.concatenate([beside(top, swapped(top)), beside(swapped(low), low)], axis=0), transfer
    )


def swap8(tiles):
    tiles = list(tiles)
    sub = lax.broadcasted_iota(jnp.int32, tiles[0].shape, 0)
    for d in (4, 2, 1):
        keep = (sub & d) == 0
        for i in range(SUB):
            if not i & d:
                a, b = tiles[i], tiles[i + d]
                tiles[i] = jnp.where(keep, a, pltpu.roll(b, d, 0))
                tiles[i + d] = jnp.where(keep, pltpu.roll(a, SUB - d, 0), b)
    return tiles


def eight(n):
    return slice(SUB * n, SUB * (n + 1))


def unpack_both(left, right, store):
    for q in range(NB):
        rows = []
        for k in range(SUB // 2 * q, SUB // 2 * (q + 1)):
            a, b = left(k), right(k)
            rows += [beside(a, swapped(b)), beside(swapped(a), b)]
        for b, tile in enumerate(swap8(rows)):
            store(b, q, tile)


def lanes_of(k):
    return slice(k * WIDE, (k + 1) * WIDE)


def unpack_trees(left_ref, right_ref, out_ref, count):
    for g in range(count // SUB):

        def store(b, q, tile):
            at = (SUB * g + b) * RANK + SUB * q
            out_ref[at : at + SUB, :] = tile

        unpack_both(
            lambda k: left_ref[0, eight(g), lanes_of(k)],
            lambda k: right_ref[0, eight(g), lanes_of(k)],
            store,
        )


def tree_kernel(
    count,
    row_order_in,
    col_order_in,
    row_bases_in,
    col_bases_in,
    row_transfer_in,
    col_transfer_in,
    leaf_gram,
    row_pay,
    col_pay,
    high,
    row_bases,
    col_bases,
    row_transfer,
    col_transfer,
    row_order,
    col_order,
    basis,
    trans,
    sems,
):
    copies = [
        pltpu.make_async_copy(source, target, sems.at[n])
        for n, (source, target) in enumerate(
            (
                (row_bases_in, row_bases),
                (col_bases_in, col_bases),
                (row_transfer_in, row_transfer),
                (col_transfer_in, col_transfer),
                (row_order_in, row_order),
                (col_order_in, col_order),
            )
        )
    ]
    for copy in copies:
        copy.start()
    copies[0].wait()
    copies[1].wait()
    unpack_trees(row_bases, col_bases, basis, count)
    for leaf in range(count):
        u = basis[leaf * RANK : (leaf + 1) * RANK, :]
        leaf_gram[leaf * RANK : (leaf + 1) * RANK, :] = dot_both(
            jnp.concatenate([u, u], axis=0).T, u
        )
    for copy in copies[2:]:
        copy.wait()
    unpack_trees(row_transfer, col_transfer, trans, 2 * count)
    nodes = []
    for q in range(count // 2):
        total = None
        for p in (2 * q, 2 * q + 1):
            r = pl.ds(pl.multiple_of(row_order[0, 0, p] * RANK, RANK), RANK)
            c = pl.ds(pl.multiple_of(col_order[0, 0, p] * RANK, RANK), RANK)
            term = sandwich_both(
                beside(leaf_gram[r, :], leaf_gram[c, :]), beside(trans[r, :], trans[c, :])
            )
            total = term if total is None else total + term
        nodes.append(total)
    offset = count
    while len(nodes) > 1:
        terms = []
        for q, gram in enumerate(nodes):
            terms.append(
                sandwich_both(gram, trans[(offset + q) * RANK : (offset + q + 1) * RANK, :])
            )
        offset += len(nodes)
        nodes = [terms[2 * q] + terms[2 * q + 1] for q in range(len(terms) // 2)]
    gram = nodes[0]
    term = sandwich_both(gram, trans[offset * RANK : (offset + 1) * RANK, :])
    first = trans[(offset + 1) * RANK : (offset + 2) * RANK, :]
    high[...] = gram
    row_pay[0:RANK, :] = beside(term, swapped(first))
    row_pay[RANK:WIDE, :] = gram
    col_pay[0:RANK, :] = beside(swapped(term), first)
    col_pay[RANK:WIDE, :] = swapped(gram)


def step_kernel(levels, top, sizes, held, apart, extra, own, recv, high_in, *refs):
    refs = list(refs)
    before = refs.pop(0) if extra else None
    high_out = refs.pop(0)
    roots_out = refs.pop() if apart else None
    pay_out = refs.pop(0) if refs else None
    nr, nc = sizes
    i, j = lax.axis_index("row"), lax.axis_index("col")
    base = 0
    if extra:
        pay_out[0:RANK, :] = before[0:RANK, :]
        base = RANK
    high = high_in[...]
    uppers = []
    for slot, (name, level) in enumerate(levels):
        d = i * nc + j if name == "r" else j * nr + i
        span = 1 << level
        upper = lax.rem(lax.div(d, span), 2) == 1
        uppers.append(upper)
        take = lax.rem(d, 2 * span) == span
        if level == top:
            take = jnp.logical_or(take, d == 0)
        mine = own[slot * RANK : (slot + 1) * RANK, :]
        theirs = recv[slot * RANK : (slot + 1) * RANK, :]
        total = mine + theirs
        if level < top:
            transfer = jnp.where(upper, mine, theirs)
            first = jnp.where(upper, theirs, mine)
            x = dot3(transfer.T[RANK:], total[:, :RANK])
            pay_out[base : base + RANK, :] = beside(swapped(dot3(x, transfer)), first)
            base += RANK
        picked = beside(total, high) if name == "r" else beside(high, swapped(total))
        high = jnp.where(take, picked, high)
    high_out[...] = high
    if extra:
        pay_out[base : base + RANK, :] = before[RANK:WIDE, :]
    if held:
        upper = uppers[0]
        start = len(levels) * RANK
        if roots_out is None:
            roots_out = pay_out.at[base:, :]
        if held == 1:
            mine = own[start : start + RANK, :]
            theirs = recv[start : start + RANK, :]
            roots_out[0:RANK, :] = jnp.where(
                upper, beside(theirs, swapped(mine)), beside(mine, swapped(theirs))
            )
        else:
            rows = held // 2 * RANK
            mine = own[start : start + rows, :]
            theirs = recv[start : start + rows, :]
            roots_out[0:rows, :] = jnp.where(upper, theirs, mine)
            roots_out[rows : 2 * rows, :] = jnp.where(upper, mine, theirs)


def chol_lanes(a_ref, r_ref):
    sub = lax.broadcasted_iota(jnp.int32, (SUB, WIDE), 0)

    def at(q):
        return slice(SUB * q, SUB * (q + 1))

    def spread(i, j):
        return r_ref[i, pl.ds(j, SUB, stride=0), :]

    def less(value, f, row):
        return lax.sub(value, lax.mul(f, row))

    for p in range(NB):
        i0 = SUB * p
        acc = [a_ref[i0 + r, at(p), :] for r in range(SUB)]
        scale = []
        for r in range(SUB):
            inv = lax.rsqrt(jnp.broadcast_to(acc[r][r : r + 1, :], (SUB, WIDE)))
            scale.append(inv)
            row = jnp.where(sub >= r, acc[r] * inv, 0.0)
            r_ref[i0 + r, at(p), :] = row
            for r2 in range(r + 1, SUB):
                acc[r2] = less(acc[r2], jnp.broadcast_to(row[r2 : r2 + 1, :], (SUB, WIDE)), row)
        for q in range(p + 1, NB):
            x = [a_ref[i0 + r, at(q), :] for r in range(SUB)]
            for r in range(SUB):
                x[r] = lax.mul(x[r], scale[r])
                r_ref[i0 + r, at(q), :] = x[r]
                for r2 in range(r + 1, SUB):
                    x[r2] = less(x[r2], spread(i0 + r, i0 + r2), x[r])
        for pi in range(p + 1, NB):
            for q0 in range(pi, NB, 2):
                qs = range(q0, min(q0 + 2, NB))
                acc2 = {(r, q): a_ref[SUB * pi + r, at(q), :] for r in range(SUB) for q in qs}
                for k in range(SUB):
                    rows = {q: r_ref[i0 + k, at(q), :] for q in qs}
                    for r in range(SUB):
                        f = spread(i0 + k, SUB * pi + r)
                        for q in qs:
                            acc2[r, q] = less(acc2[r, q], f, rows[q])
                for (r, q), value in acc2.items():
                    a_ref[SUB * pi + r, at(q), :] = value


def put_row(a_ref, i, rows):
    b0 = SUB * (i // SUB)
    t = rows.T
    a_ref[i, b0:RANK, 0 : 2 * rows.shape[0]] = jnp.concatenate([t[b0:RANK], t[RANK + b0 :]], axis=1)


def get_row(r_ref, i, count):
    b0 = SUB * (i // SUB)
    parts = []
    for half in range(2):
        if b0:
            parts.append(jnp.zeros((b0, count), F32))
        parts.append(r_ref[i, b0:RANK, half * count : (half + 1) * count])
    return jnp.concatenate(parts, axis=0).T


def chol_table_kernel(count, shapes, *refs):
    inputs = refs[: len(shapes)]
    left, right, a_ref, r_ref = refs[len(shapes) : len(shapes) + 4]
    slots = [(ref, s) for ref in inputs for s in range(ref.shape[0] // RANK)]
    slots += [slots[-1]] * (count - len(slots))
    for q in range(NB):
        groups = []
        for g in range(count // SUB):
            groups.append(
                swap8(
                    [
                        ref[s * RANK + SUB * q : s * RANK + SUB * (q + 1), :]
                        for ref, s in slots[SUB * g : SUB * (g + 1)]
                    ]
                )
            )
        for r in range(SUB):
            put_row(a_ref, SUB * q + r, jnp.concatenate([tiles[r] for tiles in groups], axis=0))
    chol_lanes(a_ref, r_ref)
    keep = lane_half(2 * SUB)
    for q in range(0, NB, 2):
        rows = [get_row(r_ref, SUB * q + r, count) for r in range(2 * SUB)]
        for g in range(count // SUB):
            upper = swap8([row[eight(g)] for row in rows[:SUB]])
            lower = swap8([row[eight(g)] for row in rows[SUB:]])
            for b in range(SUB):
                both = jnp.concatenate([upper[b], lower[b]], axis=0)
                other = swapped(both)
                for n, here, there in (
                    (SUB * g + b, both, other),
                    (count + SUB * g + b, other, both),
                ):
                    at = n * WIDE + SUB * q
                    for table, value in (
                        (left, jnp.where(keep, here, 0.0)),
                        (right, jnp.where(keep, 0.0, there)),
                    ):
                        high, low = split(value)
                        table[at : at + 2 * SUB, :] = high
                        table[at + RANK : at + RANK + 2 * SUB, :] = low


def final_kernel(high, row_out, col_out, a_ref, r_ref):
    for i in range(RANK):
        put_row(a_ref, i, jnp.broadcast_to(high[i : i + 1, :], (SUB, WIDE)))
    chol_lanes(a_ref, r_ref)
    for k in range(RANK // 2):
        even = get_row(r_ref, 2 * k, SUB)
        odd = get_row(r_ref, 2 * k + 1, SUB)
        row_out[0, 0:1, lanes_of(k)] = beside(even, swapped(odd))[0:1]
        col_out[0, 0:1, lanes_of(k)] = beside(swapped(even), odd)[0:1]


def couple_kernel(pairs, left_of, right_of, left_pick, right_pick, left, right, blocks, out, s_ref, y_ref):
    def group(g, carry):
        start = pl.multiple_of(g * 2 * SUB, 2 * SUB)

        def slab(k):
            return blocks[0, pl.ds(start, 2 * SUB), lanes_of(k)].astype(F32)

        def keep(b, q, tile):
            s_ref[b * RANK + SUB * q : b * RANK + SUB * (q + 1), :] = tile

        unpack_both(lambda k: slab(k)[:SUB], lambda k: slab(k)[SUB:], keep)

        def entry(table, pick, ref, b):
            return table[pl.ds(pl.multiple_of(pick(ref, start + b) * WIDE, WIDE), WIDE), :]

        for b in range(SUB):
            block = s_ref[b * RANK : (b + 1) * RANK, :].astype(BF16)
            rows = jnp.concatenate(
                [entry(left, left_of, left_pick, n)[:, :RANK] for n in (b, b + SUB)], axis=0
            )
            x = dot(rows, block)
            x = beside(x[:RANK], x[WIDE : WIDE + RANK]) + beside(
                x[RANK:WIDE], x[WIDE + RANK :]
            )
            first = entry(left, right_of, right_pick, b)
            second = entry(right, right_of, right_pick, b + SUB)
            weights = jnp.concatenate(
                [first[:RANK], second[:RANK], first[RANK:], second[RANK:]], axis=0
            )
            y = dot(stacked(x), weights, 1)
            y = y[:RANK] + y[RANK:]
            y_ref[b * RANK : (b + 1) * RANK, :] = y[:, :WIDE] + y[:, WIDE:]
        for q in range(NB):
            rows = swap8(
                [y_ref[b * RANK + SUB * q : b * RANK + SUB * (q + 1), :] for b in range(SUB)]
            )
            for k in range(SUB // 2):
                even, odd = rows[2 * k], rows[2 * k + 1]
                at = lanes_of(SUB // 2 * q + k)
                out[0, pl.ds(start, SUB), at] = beside(even, swapped(odd))
                out[0, pl.ds(pl.multiple_of(start + SUB, SUB), SUB), at] = beside(
                    swapped(even), odd
                )
        return carry

    lax.fori_loop(0, pairs // (2 * SUB), group, 0)


def shape(*dims):
    return jax.ShapeDtypeStruct(dims, F32)


def scratch(rows, lanes=WIDE):
    return pltpu.VMEM((rows, lanes), F32)


def call(kernel, outs, specs, scratches=(), limit=8):
    return pl.pallas_call(
        kernel,
        out_shape=outs,
        in_specs=specs,
        out_specs=jax.tree.map(lambda _: VMEM, outs),
        scratch_shapes=list(scratches),
        compiler_params=pltpu.CompilerParams(vmem_limit_bytes=limit << 20),
    )


def partner(value, axis, bit):
    return lax.ppermute(value, axis, [(i, i ^ 1 << bit) for i in range(lax.axis_size(axis))])


def body(
    row_bases,
    col_bases,
    row_transfer,
    col_transfer,
    row_order,
    col_order,
    leaf_pattern,
    leaf_blocks,
    root_rows,
    root_cols,
    root_blocks,
):
    count = row_bases.shape[1]
    nr, nc = lax.axis_size("row"), lax.axis_size("col")
    lr, lc = nr.bit_length() - 1, nc.bit_length() - 1
    top = lr + lc - 1

    leaf_gram, row_pay, col_pay, high = call(
        functools.partial(tree_kernel, count),
        [shape(count * RANK, WIDE), shape(WIDE, WIDE), shape(WIDE, WIDE), shape(RANK, WIDE)],
        [pl.BlockSpec(memory_space=pltpu.HBM)] * 6,
        [pltpu.VMEM(x.shape, F32) for x in (row_bases, col_bases, row_transfer, col_transfer)]
        + [pltpu.SMEM(x.shape, jnp.int32) for x in (row_order, col_order)]
        + [scratch(count * RANK), scratch(2 * count * RANK), pltpu.SemaphoreType.DMA((6,))],
    )(row_order, col_order, row_bases, col_bases, row_transfer, col_transfer)

    def step(levels, pay, axis, bit, high, held=0, apart=False, extra=None):
        recv = partner(pay, axis, bit)
        rows = sum(level < top for _, level in levels) * RANK
        rows += 0 if apart else held * RANK
        rows += 0 if extra is None else WIDE
        outs = [shape(RANK, WIDE)]
        if rows:
            outs.append(shape(rows, WIDE))
        if apart:
            outs.append(shape(held * RANK, WIDE))
        args = [pay, recv, high] + ([] if extra is None else [extra])
        result = call(
            functools.partial(step_kernel, levels, top, (nr, nc), held, apart, extra is not None),
            outs,
            [VMEM] * len(args),
            limit=2 + held // 4,
        )(*args)
        return result

    pay = col_pay
    for h in range(lr):
        done = h == lr - 1
        high, pay, *rest = step(
            [("c", h)],
            pay,
            "row",
            h,
            high,
            held=1 << h,
            apart=done,
            extra=row_pay if done else None,
        )
    col_roots = rest[0]
    for h in range(lc):
        done = h == lc - 1
        high, pay, *rest = step(
            [("r", h), ("c", lr + h)], pay, "col", h, high, held=1 << h, apart=done
        )
    row_roots = rest[0]
    for h in range(lr):
        high, *rest = step([("r", lc + h)], pay, "row", h, high)
        pay = rest[0] if rest else None

    big = [pltpu.VMEM((RANK, RANK, WIDE), F32)] * 2

    def tables(count, *sources):
        out = jax.ShapeDtypeStruct((2 * count * WIDE, WIDE), BF16)
        return call(
            functools.partial(chol_table_kernel, count, [x.shape for x in sources]),
            [out, out],
            [VMEM] * len(sources),
            big,
            limit=5 + count // 3,
        )(*sources)

    def couple(left_of, right_of, left_pick, right_pick, factors, blocks):
        pairs = blocks.shape[1]
        return call(
            functools.partial(couple_kernel, pairs, left_of, right_of),
            shape(1, pairs, RANK * RANK),
            [SMEM, SMEM, VMEM, VMEM, VMEM],
            [scratch(SUB * RANK), scratch(SUB * RANK)],
        )(left_pick, right_pick, *factors, blocks)

    leaf_coupled = couple(
        lambda ref, b: ref[0, 0, b],
        lambda ref, b: ref[0, 1, b] + count,
        leaf_pattern,
        leaf_pattern,
        tables(count, leaf_gram),
        leaf_blocks,
    )
    row_slots, col_slots = nc // 2, nr // 2
    slots = -(-(row_slots + col_slots) // SUB) * SUB
    root_coupled = couple(
        lambda ref, b: (ref[0, 0, b] & 1) * slots + (ref[0, 0, b] >> 1),
        lambda ref, b: (ref[0, 0, b] & 1) * slots + (ref[0, 0, b] >> 1) + row_slots,
        root_rows,
        root_cols,
        tables(slots, row_roots, col_roots),
        root_blocks,
    )
    row_upper_r, col_upper_r = call(
        final_kernel, [shape(1, 1, RANK * RANK), shape(1, 1, RANK * RANK)], [VMEM], big
    )(high)
    return (leaf_coupled, root_coupled, row_upper_r, col_upper_r)


def solution(mesh):
    return jax.shard_map(
        body,
        mesh=mesh,
        in_specs=(
            P("row", "col", None),
            P("col", "row", None),
            P("row", "col", None),
            P("col", "row", None),
            P("row", "col", None),
            P("col", "row", None),
            P("row", "col", None),
            P("row", "col", None),
            P("row", "col", None),
            P("row", "col", None),
            P("row", "col", None),
        ),
        out_specs=(
            P("row", "col", None),
            P("row", "col", None),
            P("row", "col", None),
            P("col", "row", None),
        ),
        check_vma=False,
    )
```

```python
import functools

import jax
import jax.numpy as jnp
from jax import lax
from jax.experimental import pallas as pl
from jax.experimental.pallas import tpu as pltpu
from jax.sharding import PartitionSpec as P


RANK = 64
WIDE = 2 * RANK
SUB = 8
NB = RANK // SUB
F32 = jnp.float32
BF16 = jnp.bfloat16
VMEM = pl.BlockSpec(memory_space=pltpu.VMEM)
SMEM = pl.BlockSpec(memory_space=pltpu.SMEM)
HBM = pl.BlockSpec(memory_space=pltpu.HBM)


def split(x):
    high = x.astype(BF16)
    return high, (x - high.astype(F32)).astype(BF16)


def dot(a, b, rhs_dim=0):
    return lax.dot_general(a, b, (((1,), (rhs_dim,)), ((), ())), preferred_element_type=F32)


def dot3(a, b):
    a_high, a_low = split(a)
    b_high, b_low = split(b)
    return dot(a_high, b_high) + (dot(a_high, b_low) + dot(a_low, b_high))


def stacked(x, axis=0):
    return jnp.concatenate(split(x), axis=axis)


def lane_half(rows):
    return lax.broadcasted_iota(jnp.int32, (rows, WIDE), 1) < RANK


def swapped(x):
    return pltpu.roll(x, RANK, 1)


def beside(left, right):
    return jnp.where(lane_half(left.shape[0]), left, right)


def dot_both(a, b):
    y = dot(stacked(a), stacked(b))
    return beside(y[:RANK], y[RANK:WIDE]) + beside(y[WIDE : WIDE + RANK], y[WIDE + RANK :])


def sandwich_both(gram, transfer):
    x = dot(stacked(jnp.concatenate([transfer, transfer], axis=0).T), stacked(gram))
    x = x[:WIDE] + x[WIDE:]
    top, low = x[:RANK], x[RANK:]
    return dot_both(
        jnp.concatenate([beside(top, swapped(top)), beside(swapped(low), low)], axis=0), transfer
    )


def swap8(tiles):
    tiles = list(tiles)
    sub = lax.broadcasted_iota(jnp.int32, tiles[0].shape, 0)
    for d in (4, 2, 1):
        keep = (sub & d) == 0
        for i in range(SUB):
            if not i & d:
                a, b = tiles[i], tiles[i + d]
                tiles[i] = jnp.where(keep, a, pltpu.roll(b, d, 0))
                tiles[i + d] = jnp.where(keep, pltpu.roll(a, SUB - d, 0), b)
    return tiles


def eight(n):
    return slice(SUB * n, SUB * (n + 1))


def unpack_both(left, right, store):
    for q in range(NB):
        rows = []
        for k in range(SUB // 2 * q, SUB // 2 * (q + 1)):
            a, b = left(k), right(k)
            rows += [beside(a, swapped(b)), beside(swapped(a), b)]
        for b, tile in enumerate(swap8(rows)):
            store(b, q, tile)


def lanes_of(k):
    return slice(k * WIDE, (k + 1) * WIDE)


def unpack_trees(left_ref, right_ref, out_ref, count):
    for g in range(count // SUB):

        def store(b, q, tile):
            at = (SUB * g + b) * RANK + SUB * q
            out_ref[at : at + SUB, :] = tile

        unpack_both(
            lambda k: left_ref[0, eight(g), lanes_of(k)],
            lambda k: right_ref[0, eight(g), lanes_of(k)],
            store,
        )


def tree_kernel(
    count,
    row_order_in,
    col_order_in,
    row_bases_in,
    col_bases_in,
    row_transfer_in,
    col_transfer_in,
    leaf_gram,
    row_pay,
    col_pay,
    high,
    row_bases,
    col_bases,
    row_transfer,
    col_transfer,
    row_order,
    col_order,
    basis,
    trans,
    sems,
):
    copies = [
        pltpu.make_async_copy(source, target, sems.at[n])
        for n, (source, target) in enumerate(
            (
                (row_bases_in, row_bases),
                (col_bases_in, col_bases),
                (row_transfer_in, row_transfer),
                (col_transfer_in, col_transfer),
                (row_order_in, row_order),
                (col_order_in, col_order),
            )
        )
    ]
    for copy in copies:
        copy.start()
    copies[0].wait()
    copies[1].wait()
    unpack_trees(row_bases, col_bases, basis, count)
    for leaf in range(count):
        u = basis[leaf * RANK : (leaf + 1) * RANK, :]
        leaf_gram[leaf * RANK : (leaf + 1) * RANK, :] = dot_both(
            jnp.concatenate([u, u], axis=0).T, u
        )
    for copy in copies[2:]:
        copy.wait()
    unpack_trees(row_transfer, col_transfer, trans, 2 * count)
    nodes = []
    for q in range(count // 2):
        total = None
        for p in (2 * q, 2 * q + 1):
            r = pl.ds(pl.multiple_of(row_order[0, 0, p] * RANK, RANK), RANK)
            c = pl.ds(pl.multiple_of(col_order[0, 0, p] * RANK, RANK), RANK)
            term = sandwich_both(
                beside(leaf_gram[r, :], leaf_gram[c, :]), beside(trans[r, :], trans[c, :])
            )
            total = term if total is None else total + term
        nodes.append(total)
    offset = count
    while len(nodes) > 1:
        terms = []
        for q, gram in enumerate(nodes):
            terms.append(
                sandwich_both(gram, trans[(offset + q) * RANK : (offset + q + 1) * RANK, :])
            )
        offset += len(nodes)
        nodes = [terms[2 * q] + terms[2 * q + 1] for q in range(len(terms) // 2)]
    gram = nodes[0]
    term = sandwich_both(gram, trans[offset * RANK : (offset + 1) * RANK, :])
    first = trans[(offset + 1) * RANK : (offset + 2) * RANK, :]
    high[...] = gram
    row_pay[0:RANK, :] = beside(term, swapped(first))
    row_pay[RANK:WIDE, :] = gram
    col_pay[0:RANK, :] = beside(swapped(term), first)
    col_pay[RANK:WIDE, :] = swapped(gram)


def step_kernel(levels, top, sizes, held, apart, extra, own, recv, high_in, *refs):
    refs = list(refs)
    before = refs.pop(0) if extra else None
    high_out = refs.pop(0)
    roots_out = refs.pop() if apart else None
    pay_out = refs.pop(0) if refs else None
    nr, nc = sizes
    i, j = lax.axis_index("row"), lax.axis_index("col")
    base = 0
    if extra:
        pay_out[0:RANK, :] = before[0:RANK, :]
        base = RANK
    high = high_in[...]
    uppers = []
    for slot, (name, level) in enumerate(levels):
        d = i * nc + j if name == "r" else j * nr + i
        span = 1 << level
        upper = lax.rem(lax.div(d, span), 2) == 1
        uppers.append(upper)
        take = lax.rem(d, 2 * span) == span
        if level == top:
            take = jnp.logical_or(take, d == 0)
        mine = own[slot * RANK : (slot + 1) * RANK, :]
        theirs = recv[slot * RANK : (slot + 1) * RANK, :]
        total = mine + theirs
        if level < top:
            transfer = jnp.where(upper, mine, theirs)
            first = jnp.where(upper, theirs, mine)
            x = dot3(transfer.T[RANK:], total[:, :RANK])
            pay_out[base : base + RANK, :] = beside(swapped(dot3(x, transfer)), first)
            base += RANK
        picked = beside(total, high) if name == "r" else beside(high, swapped(total))
        high = jnp.where(take, picked, high)
    high_out[...] = high
    if extra:
        pay_out[base : base + RANK, :] = before[RANK:WIDE, :]
    if held:
        upper = uppers[0]
        start = len(levels) * RANK
        if roots_out is None:
            roots_out = pay_out.at[base:, :]
        if held == 1:
            mine = own[start : start + RANK, :]
            theirs = recv[start : start + RANK, :]
            roots_out[0:RANK, :] = jnp.where(
                upper, beside(theirs, swapped(mine)), beside(mine, swapped(theirs))
            )
        else:
            rows = held // 2 * RANK
            mine = own[start : start + rows, :]
            theirs = recv[start : start + rows, :]
            roots_out[0:rows, :] = jnp.where(upper, theirs, mine)
            roots_out[rows : 2 * rows, :] = jnp.where(upper, mine, theirs)


def chol_lanes(a_ref, r_ref, scale_ref):
    sub = lax.broadcasted_iota(jnp.int32, (SUB, WIDE), 0)
    here = lax.axis_index("row") >= 0

    def spread(i, j):
        return r_ref[i, pl.ds(j, SUB, stride=0), :]

    def less(value, f, row):
        return lax.sub(value, lax.mul(f, row))

    def reduced(p, qs):
        acc = {(r, q): a_ref[SUB * p + r, eight(q), :] for r in range(SUB) for q in qs}
        for k in range(SUB * p):
            rows = [r_ref[k, eight(q), :] for q in qs]
            for r in range(SUB):
                f = spread(k, SUB * p + r)
                for q, row in zip(qs, rows):
                    acc[r, q] = less(acc[r, q], f, row)
        return acc

    def diagonal(p):
        acc = reduced(p, [p])
        for r in range(SUB):
            inv = lax.rsqrt(jnp.broadcast_to(acc[r, p][r : r + 1, :], (SUB, WIDE)))
            scale_ref[SUB * p + r] = inv
            row = jnp.where(sub >= r, lax.mul(acc[r, p], inv), 0.0)
            r_ref[SUB * p + r, eight(p), :] = row
            for r2 in range(r + 1, SUB):
                f = jnp.broadcast_to(row[r2 : r2 + 1, :], (SUB, WIDE))
                acc[r2, p] = less(acc[r2, p], f, row)

    def beyond(p, qs):
        acc = reduced(p, qs)
        for r in range(SUB):
            inv = scale_ref[SUB * p + r]
            for q in qs:
                acc[r, q] = lax.mul(acc[r, q], inv)
                r_ref[SUB * p + r, eight(q), :] = acc[r, q]
            for r2 in range(r + 1, SUB):
                f = spread(SUB * p + r, SUB * p + r2)
                for q in qs:
                    acc[r2, q] = less(acc[r2, q], f, acc[r, q])

    for p in range(-1, NB - 1):

        @pl.when(here)
        def _():
            if p >= 0:
                beyond(p, [p + 1])
            diagonal(p + 1)
            for q in range(p + 2, NB, 2):
                if p >= 0:
                    beyond(p, list(range(q, min(q + 2, NB))))


def put_row(a_ref, i, rows):
    b0 = SUB * (i // SUB)
    t = rows.T
    a_ref[i, b0:RANK, 0 : 2 * rows.shape[0]] = jnp.concatenate([t[b0:RANK], t[RANK + b0 :]], axis=1)


def get_row(r_ref, i, count):
    b0 = SUB * (i // SUB)
    parts = []
    for half in range(2):
        if b0:
            parts.append(jnp.zeros((b0, count), F32))
        parts.append(r_ref[i, b0:RANK, half * count : (half + 1) * count])
    return jnp.concatenate(parts, axis=0).T


def chol_table_kernel(count, shapes, *refs):
    inputs = refs[: len(shapes)]
    left, right, a_ref, r_ref, scale_ref = refs[len(shapes) : len(shapes) + 5]
    slots = [(ref, s) for ref in inputs for s in range(ref.shape[0] // RANK)]
    slots += [slots[-1]] * (count - len(slots))
    for q in range(NB):
        groups = []
        for g in range(count // SUB):
            groups.append(
                swap8(
                    [
                        ref[s * RANK + SUB * q : s * RANK + SUB * (q + 1), :]
                        for ref, s in slots[SUB * g : SUB * (g + 1)]
                    ]
                )
            )
        for r in range(SUB):
            put_row(a_ref, SUB * q + r, jnp.concatenate([tiles[r] for tiles in groups], axis=0))
    chol_lanes(a_ref, r_ref, scale_ref)
    keep = lane_half(2 * SUB)
    for q in range(0, NB, 2):
        rows = [get_row(r_ref, SUB * q + r, count) for r in range(2 * SUB)]
        for g in range(count // SUB):
            upper = swap8([row[eight(g)] for row in rows[:SUB]])
            lower = swap8([row[eight(g)] for row in rows[SUB:]])
            for b in range(SUB):
                both = jnp.concatenate([upper[b], lower[b]], axis=0)
                other = swapped(both)
                for n, here, there in (
                    (SUB * g + b, both, other),
                    (count + SUB * g + b, other, both),
                ):
                    at = n * WIDE + SUB * q
                    for table, value in (
                        (left, jnp.where(keep, here, 0.0)),
                        (right, jnp.where(keep, 0.0, there)),
                    ):
                        high, low = split(value)
                        table[at : at + 2 * SUB, :] = high
                        table[at + RANK : at + RANK + 2 * SUB, :] = low


def final_kernel(high, row_out, col_out, a_ref, r_ref, scale_ref):
    for i in range(RANK):
        b0 = SUB * (i // SUB)
        value = high[b0:RANK, :]
        a_ref[i, b0:RANK, :] = pltpu.roll(value, WIDE - i, 1) if i else value
    chol_lanes(a_ref, r_ref, scale_ref)
    lane = lax.broadcasted_iota(jnp.int32, (SUB, WIDE), 1) % RANK
    columns = []
    for q in range(NB):
        tile = jnp.zeros((SUB, WIDE), F32)
        for i in range(SUB * (q + 1)):
            value = r_ref[i, eight(q), :]
            tile = jnp.where(lane == i, pltpu.roll(value, i, 1) if i else value, tile)
        columns.append(tile)
    columns = jnp.concatenate(columns, axis=0)
    rows = jnp.concatenate([columns, columns], axis=0).T
    for out, half in ((row_out, rows[:RANK]), (col_out, rows[RANK:])):
        for k in range(RANK // 2):
            out[0, 0:1, lanes_of(k)] = beside(half[2 * k : 2 * k + 1], half[2 * k + 1 : 2 * k + 2])


def couple_kernel(
    first_group, groups, left_of, right_of, left_pick, right_pick, left, right, blocks, *refs
):
    target, s_ref, y_ref, out, sem = refs[-5:]

    def copy(g):
        at = pl.ds(pl.multiple_of(g * 2 * SUB, 2 * SUB), 2 * SUB)
        to = pl.ds(pl.multiple_of((first_group + g) * 2 * SUB, 2 * SUB), 2 * SUB)
        return pltpu.make_async_copy(out.at[at, :], target.at[0, to, :], sem.at[g])

    def group(g, carry):
        local = pl.multiple_of(g * 2 * SUB, 2 * SUB)
        start = pl.multiple_of((first_group + g) * 2 * SUB, 2 * SUB)

        def slab(k):
            return blocks[0, pl.ds(start, 2 * SUB), lanes_of(k)].astype(F32)

        def keep(b, q, tile):
            s_ref[b * RANK + SUB * q : b * RANK + SUB * (q + 1), :] = tile

        unpack_both(lambda k: slab(k)[:SUB], lambda k: slab(k)[SUB:], keep)

        def entry(table, pick, ref, b):
            return table[pl.ds(pl.multiple_of(pick(ref, start + b) * WIDE, WIDE), WIDE), :]

        for b in range(SUB):
            block = s_ref[b * RANK : (b + 1) * RANK, :].astype(BF16)
            rows = jnp.concatenate(
                [entry(left, left_of, left_pick, n)[:, :RANK] for n in (b, b + SUB)], axis=0
            )
            x = dot(rows, block)
            x = beside(x[:RANK], x[WIDE : WIDE + RANK]) + beside(
                x[RANK:WIDE], x[WIDE + RANK :]
            )
            first = entry(left, right_of, right_pick, b)
            second = entry(right, right_of, right_pick, b + SUB)
            weights = jnp.concatenate(
                [first[:RANK], second[:RANK], first[RANK:], second[RANK:]], axis=0
            )
            y = dot(stacked(x), weights, 1)
            y = y[:RANK] + y[RANK:]
            y_ref[b * RANK : (b + 1) * RANK, :] = y[:, :WIDE] + y[:, WIDE:]
        for q in range(NB):
            rows = swap8(
                [y_ref[b * RANK + SUB * q : b * RANK + SUB * (q + 1), :] for b in range(SUB)]
            )
            for k in range(SUB // 2):
                even, odd = rows[2 * k], rows[2 * k + 1]
                at = lanes_of(SUB // 2 * q + k)
                out[pl.ds(local, SUB), at] = beside(even, swapped(odd))
                out[pl.ds(pl.multiple_of(local + SUB, SUB), SUB), at] = beside(
                    swapped(even), odd
                )
        copy(g).start()
        return carry

    lax.fori_loop(0, groups, group, 0)
    for g in range(groups):
        copy(g).wait()


def shape(*dims):
    return jax.ShapeDtypeStruct(dims, F32)


def scratch(rows, lanes=WIDE):
    return pltpu.VMEM((rows, lanes), F32)


def call(kernel, outs, specs, scratches=(), limit=8):
    return pl.pallas_call(
        kernel,
        out_shape=outs,
        in_specs=specs,
        out_specs=jax.tree.map(lambda _: VMEM, outs),
        scratch_shapes=list(scratches),
        compiler_params=pltpu.CompilerParams(vmem_limit_bytes=limit << 20),
    )


def partner(value, axis, bit):
    return lax.ppermute(value, axis, [(i, i ^ 1 << bit) for i in range(lax.axis_size(axis))])


def body(
    row_bases,
    col_bases,
    row_transfer,
    col_transfer,
    row_order,
    col_order,
    leaf_pattern,
    leaf_blocks,
    root_rows,
    root_cols,
    root_blocks,
):
    count = row_bases.shape[1]
    nr, nc = lax.axis_size("row"), lax.axis_size("col")
    lr, lc = nr.bit_length() - 1, nc.bit_length() - 1
    top = lr + lc - 1

    leaf_gram, row_pay, col_pay, high = call(
        functools.partial(tree_kernel, count),
        [shape(count * RANK, WIDE), shape(WIDE, WIDE), shape(WIDE, WIDE), shape(RANK, WIDE)],
        [HBM] * 6,
        [pltpu.VMEM(x.shape, F32) for x in (row_bases, col_bases, row_transfer, col_transfer)]
        + [pltpu.SMEM(x.shape, jnp.int32) for x in (row_order, col_order)]
        + [scratch(count * RANK), scratch(2 * count * RANK), pltpu.SemaphoreType.DMA((6,))],
    )(
        *(
            pltpu.with_memory_space_constraint(x, pltpu.HBM)
            for x in (row_order, col_order, row_bases, col_bases, row_transfer, col_transfer)
        )
    )

    def step(levels, pay, axis, bit, high, held=0, apart=False, extra=None):
        recv = partner(pay, axis, bit)
        rows = sum(level < top for _, level in levels) * RANK
        rows += 0 if apart else held * RANK
        rows += 0 if extra is None else WIDE
        outs = [shape(RANK, WIDE)]
        if rows:
            outs.append(shape(rows, WIDE))
        if apart:
            outs.append(shape(held * RANK, WIDE))
        args = [pay, recv, high] + ([] if extra is None else [extra])
        result = call(
            functools.partial(step_kernel, levels, top, (nr, nc), held, apart, extra is not None),
            outs,
            [VMEM] * len(args),
            limit=2 + held // 4,
        )(*args)
        return result

    pay = col_pay
    for h in range(lr):
        done = h == lr - 1
        high, pay, *rest = step(
            [("c", h)],
            pay,
            "row",
            h,
            high,
            held=1 << h,
            apart=done,
            extra=row_pay if done else None,
        )
    col_roots = rest[0]
    for h in range(lc):
        done = h == lc - 1
        high, pay, *rest = step(
            [("r", h), ("c", lr + h)], pay, "col", h, high, held=1 << h, apart=done
        )
    row_roots = rest[0]
    for h in range(lr):
        high, *rest = step([("r", lc + h)], pay, "row", h, high)
        pay = rest[0] if rest else None

    big = [pltpu.VMEM((RANK, RANK, WIDE), F32)] * 2 + [pltpu.VMEM((RANK, SUB, WIDE), F32)]

    def tables(count, *sources):
        out = jax.ShapeDtypeStruct((2 * count * WIDE, WIDE), BF16)
        return call(
            functools.partial(chol_table_kernel, count, [x.shape for x in sources]),
            [out, out],
            [VMEM] * len(sources),
            big,
            limit=5 + count // 3,
        )(*sources)

    def couple(parts, left_of, right_of, left_pick, right_pick, factors, blocks):
        result, first = [], 0
        for groups in parts:
            pairs = groups * 2 * SUB
            result = [
                pl.pallas_call(
                    functools.partial(couple_kernel, first, groups, left_of, right_of),
                    out_shape=shape(1, blocks.shape[1], RANK * RANK),
                    in_specs=[SMEM, SMEM, VMEM, VMEM, VMEM] + [HBM] * len(result),
                    out_specs=HBM,
                    scratch_shapes=[
                        scratch(SUB * RANK),
                        scratch(SUB * RANK),
                        scratch(pairs, RANK * RANK),
                        pltpu.SemaphoreType.DMA((groups,)),
                    ],
                    input_output_aliases={5: 0} if result else {},
                    compiler_params=pltpu.CompilerParams(vmem_limit_bytes=6 << 20),
                )(left_pick, right_pick, *factors, blocks, *result)
            ]
            first += groups
        return result[0]

    leaf_groups = leaf_blocks.shape[1] // (2 * SUB)
    root_groups = root_blocks.shape[1] // (2 * SUB)
    leaf_coupled = couple(
        (leaf_groups // 2, leaf_groups - leaf_groups // 2),
        lambda ref, b: ref[0, 0, b],
        lambda ref, b: ref[0, 1, b] + count,
        leaf_pattern,
        leaf_pattern,
        tables(count, leaf_gram),
        leaf_blocks,
    )
    row_slots, col_slots = nc // 2, nr // 2
    slots = -(-(row_slots + col_slots) // SUB) * SUB
    root_coupled = couple(
        (root_groups,),
        lambda ref, b: (ref[0, 0, b] & 1) * slots + (ref[0, 0, b] >> 1),
        lambda ref, b: (ref[0, 0, b] & 1) * slots + (ref[0, 0, b] >> 1) + row_slots,
        root_rows,
        root_cols,
        tables(slots, row_roots, col_roots),
        root_blocks,
    )
    row_upper_r, col_upper_r = call(
        final_kernel, [shape(1, 1, RANK * RANK), shape(1, 1, RANK * RANK)], [VMEM], big
    )(high)
    return (leaf_coupled, root_coupled, row_upper_r, col_upper_r)


def solution(mesh):
    return jax.shard_map(
        body,
        mesh=mesh,
        in_specs=(
            P("row", "col", None),
            P("col", "row", None),
            P("row", "col", None),
            P("col", "row", None),
            P("row", "col", None),
            P("col", "row", None),
            P("row", "col", None),
            P("row", "col", None),
            P("row", "col", None),
            P("row", "col", None),
            P("row", "col", None),
        ),
        out_specs=(
            P("row", "col", None),
            P("row", "col", None),
            P("row", "col", None),
            P("col", "row", None),
        ),
        check_vma=False,
    )
```

```python
import functools

import jax
import jax.numpy as jnp
from jax import lax
from jax.experimental import pallas as pl
from jax.experimental.pallas import tpu as pltpu
from jax.sharding import PartitionSpec as P


RANK = 64
WIDE = 2 * RANK
SUB = 8
NB = RANK // SUB
F32 = jnp.float32
BF16 = jnp.bfloat16
VMEM = pl.BlockSpec(memory_space=pltpu.VMEM)
SMEM = pl.BlockSpec(memory_space=pltpu.SMEM)
HBM = pl.BlockSpec(memory_space=pltpu.HBM)


def split(x):
    high = x.astype(BF16)
    return high, (x - high.astype(F32)).astype(BF16)


def dot(a, b, rhs_dim=0):
    return lax.dot_general(a, b, (((1,), (rhs_dim,)), ((), ())), preferred_element_type=F32)


def dot3(a, b):
    a_high, a_low = split(a)
    b_high, b_low = split(b)
    return dot(a_high, b_high) + (dot(a_high, b_low) + dot(a_low, b_high))


def stacked(x, axis=0):
    return jnp.concatenate(split(x), axis=axis)


def lane_half(rows):
    return lax.broadcasted_iota(jnp.int32, (rows, WIDE), 1) < RANK


def swapped(x):
    return pltpu.roll(x, RANK, 1)


def beside(left, right):
    return jnp.where(lane_half(left.shape[0]), left, right)


def dot_both(a, b):
    y = dot(stacked(a), stacked(b))
    return beside(y[:RANK], y[RANK:WIDE]) + beside(y[WIDE : WIDE + RANK], y[WIDE + RANK :])


def sandwich_both(gram, transfer):
    x = dot(stacked(jnp.concatenate([transfer, transfer], axis=0).T), stacked(gram))
    x = x[:WIDE] + x[WIDE:]
    top, low = x[:RANK], x[RANK:]
    return dot_both(
        jnp.concatenate([beside(top, swapped(top)), beside(swapped(low), low)], axis=0), transfer
    )


def swap8(tiles):
    tiles = list(tiles)
    sub = lax.broadcasted_iota(jnp.int32, tiles[0].shape, 0)
    for d in (4, 2, 1):
        keep = (sub & d) == 0
        for i in range(SUB):
            if not i & d:
                a, b = tiles[i], tiles[i + d]
                tiles[i] = jnp.where(keep, a, pltpu.roll(b, d, 0))
                tiles[i + d] = jnp.where(keep, pltpu.roll(a, SUB - d, 0), b)
    return tiles


def eight(n):
    return slice(SUB * n, SUB * (n + 1))


def unpack_both(left, right, store):
    for q in range(NB):
        rows = []
        for k in range(SUB // 2 * q, SUB // 2 * (q + 1)):
            a, b = left(k), right(k)
            rows += [beside(a, swapped(b)), beside(swapped(a), b)]
        for b, tile in enumerate(swap8(rows)):
            store(b, q, tile)


def lanes_of(k):
    return slice(k * WIDE, (k + 1) * WIDE)


def unpack_trees(left_ref, right_ref, out_ref, count):
    for g in range(count // SUB):

        def store(b, q, tile):
            at = (SUB * g + b) * RANK + SUB * q
            out_ref[at : at + SUB, :] = tile

        unpack_both(
            lambda k: left_ref[0, eight(g), lanes_of(k)],
            lambda k: right_ref[0, eight(g), lanes_of(k)],
            store,
        )


def tree_kernel(
    count,
    row_order_in,
    col_order_in,
    row_bases_in,
    col_bases_in,
    row_transfer_in,
    col_transfer_in,
    *refs,
):
    picks_in, refs = refs[:3], refs[3:]
    leaf_gram, row_pay, col_pay, high = refs[:4]
    picks, refs = refs[4:7], refs[7:]
    (
        row_bases,
        col_bases,
        row_transfer,
        col_transfer,
        row_order,
        col_order,
        basis,
        trans,
        sems,
    ) = refs
    copies = [
        pltpu.make_async_copy(source, target, sems.at[n])
        for n, (source, target) in enumerate(
            (
                (row_bases_in, row_bases),
                (col_bases_in, col_bases),
                (row_transfer_in, row_transfer),
                (col_transfer_in, col_transfer),
                (row_order_in, row_order),
                (col_order_in, col_order),
                *zip(picks_in, picks),
            )
        )
    ]
    for copy in copies:
        copy.start()
    copies[0].wait()
    copies[1].wait()
    unpack_trees(row_bases, col_bases, basis, count)
    for leaf in range(count):
        u = basis[leaf * RANK : (leaf + 1) * RANK, :]
        leaf_gram[leaf * RANK : (leaf + 1) * RANK, :] = dot_both(
            jnp.concatenate([u, u], axis=0).T, u
        )
    for copy in copies[2:6]:
        copy.wait()
    unpack_trees(row_transfer, col_transfer, trans, 2 * count)
    nodes = []
    for q in range(count // 2):
        total = None
        for p in (2 * q, 2 * q + 1):
            r = pl.ds(pl.multiple_of(row_order[0, 0, p] * RANK, RANK), RANK)
            c = pl.ds(pl.multiple_of(col_order[0, 0, p] * RANK, RANK), RANK)
            term = sandwich_both(
                beside(leaf_gram[r, :], leaf_gram[c, :]), beside(trans[r, :], trans[c, :])
            )
            total = term if total is None else total + term
        nodes.append(total)
    offset = count
    while len(nodes) > 1:
        terms = []
        for q, gram in enumerate(nodes):
            terms.append(
                sandwich_both(gram, trans[(offset + q) * RANK : (offset + q + 1) * RANK, :])
            )
        offset += len(nodes)
        nodes = [terms[2 * q] + terms[2 * q + 1] for q in range(len(terms) // 2)]
    gram = nodes[0]
    term = sandwich_both(gram, trans[offset * RANK : (offset + 1) * RANK, :])
    first = trans[(offset + 1) * RANK : (offset + 2) * RANK, :]
    high[...] = gram
    row_pay[0:RANK, :] = beside(term, swapped(first))
    row_pay[RANK:WIDE, :] = gram
    col_pay[0:RANK, :] = beside(swapped(term), first)
    col_pay[RANK:WIDE, :] = swapped(gram)
    for copy in copies[6:]:
        copy.wait()


def step_kernel(levels, top, sizes, held, apart, extra, own, recv, high_in, *refs):
    refs = list(refs)
    before = refs.pop(0) if extra else None
    high_out = refs.pop(0)
    roots_out = refs.pop() if apart else None
    pay_out = refs.pop(0) if refs else None
    nr, nc = sizes
    i, j = lax.axis_index("row"), lax.axis_index("col")
    base = 0
    if extra:
        pay_out[0:RANK, :] = before[0:RANK, :]
        base = RANK
    high = high_in[...]
    uppers = []
    for slot, (name, level) in enumerate(levels):
        d = i * nc + j if name == "r" else j * nr + i
        span = 1 << level
        upper = lax.rem(lax.div(d, span), 2) == 1
        uppers.append(upper)
        take = lax.rem(d, 2 * span) == span
        if level == top:
            take = jnp.logical_or(take, d == 0)
        mine = own[slot * RANK : (slot + 1) * RANK, :]
        theirs = recv[slot * RANK : (slot + 1) * RANK, :]
        total = mine + theirs
        if level < top:
            transfer = jnp.where(upper, mine, theirs)
            first = jnp.where(upper, theirs, mine)
            x = dot3(transfer.T[RANK:], total[:, :RANK])
            pay_out[base : base + RANK, :] = beside(swapped(dot3(x, transfer)), first)
            base += RANK
        picked = beside(total, high) if name == "r" else beside(high, swapped(total))
        high = jnp.where(take, picked, high)
    high_out[...] = high
    if extra:
        pay_out[base : base + RANK, :] = before[RANK:WIDE, :]
    if held:
        upper = uppers[0]
        start = len(levels) * RANK
        if roots_out is None:
            roots_out = pay_out.at[base:, :]
        if held == 1:
            mine = own[start : start + RANK, :]
            theirs = recv[start : start + RANK, :]
            roots_out[0:RANK, :] = jnp.where(
                upper, beside(theirs, swapped(mine)), beside(mine, swapped(theirs))
            )
        else:
            rows = held // 2 * RANK
            mine = own[start : start + rows, :]
            theirs = recv[start : start + rows, :]
            roots_out[0:rows, :] = jnp.where(upper, theirs, mine)
            roots_out[rows : 2 * rows, :] = jnp.where(upper, mine, theirs)


def chol_lanes(a_ref, r_ref, scale_ref):
    sub = lax.broadcasted_iota(jnp.int32, (SUB, WIDE), 0)
    here = lax.axis_index("row") >= 0

    def spread(i, j):
        return r_ref[i, pl.ds(j, SUB, stride=0), :]

    def less(value, f, row):
        return lax.sub(value, lax.mul(f, row))

    def reduced(p, qs):
        acc = {(r, q): a_ref[SUB * p + r, eight(q), :] for r in range(SUB) for q in qs}
        for k in range(SUB * p):
            rows = [r_ref[k, eight(q), :] for q in qs]
            for r in range(SUB):
                f = spread(k, SUB * p + r)
                for q, row in zip(qs, rows):
                    acc[r, q] = less(acc[r, q], f, row)
        return acc

    def diagonal(p):
        acc = reduced(p, [p])
        for r in range(SUB):
            inv = lax.rsqrt(jnp.broadcast_to(acc[r, p][r : r + 1, :], (SUB, WIDE)))
            scale_ref[SUB * p + r] = inv
            row = jnp.where(sub >= r, lax.mul(acc[r, p], inv), 0.0)
            r_ref[SUB * p + r, eight(p), :] = row
            for r2 in range(r + 1, SUB):
                f = jnp.broadcast_to(row[r2 : r2 + 1, :], (SUB, WIDE))
                acc[r2, p] = less(acc[r2, p], f, row)

    def beyond(p, qs):
        acc = reduced(p, qs)
        for r in range(SUB):
            inv = scale_ref[SUB * p + r]
            for q in qs:
                acc[r, q] = lax.mul(acc[r, q], inv)
                r_ref[SUB * p + r, eight(q), :] = acc[r, q]
            for r2 in range(r + 1, SUB):
                f = spread(SUB * p + r, SUB * p + r2)
                for q in qs:
                    acc[r2, q] = less(acc[r2, q], f, acc[r, q])

    for p in range(-1, NB - 1):

        @pl.when(here)
        def _():
            if p >= 0:
                beyond(p, [p + 1])
            diagonal(p + 1)
            for q in range(p + 2, NB, 2):
                if p >= 0:
                    beyond(p, list(range(q, min(q + 2, NB))))


CELL = WIDE // SUB


def load_slots(slots, a_ref):
    cell = lax.broadcasted_iota(jnp.int32, (RANK, WIDE), 1) % SUB
    for q in range(NB):
        b0 = SUB * q
        turned = []
        for g in range(0, len(slots), CELL):
            group = slots[g : g + CELL]
            group = group + [group[-1]] * (CELL - len(group))
            tiles = [ref[s * RANK + b0 : s * RANK + b0 + SUB, :] for ref, s in group]
            t = jnp.concatenate(tiles, axis=0).T
            turned += [t[b0:RANK], t[RANK + b0 :]]
        for r in range(SUB):
            value = None
            for offset, t in enumerate(turned):
                t = pltpu.roll(t, (offset - r) % WIDE, 1) if offset != r else t
                value = t if value is None else jnp.where(cell[b0:] == offset, t, value)
            a_ref[b0 + r, b0:RANK, :] = value


def factor_tiles(r_ref, q, group):
    cell = lax.broadcasted_iota(jnp.int32, (SUB, WIDE), 1) % SUB
    columns = []
    for half in range(2):
        offset = 2 * group + half
        for p in range(NB):
            tile = jnp.zeros((SUB, WIDE), F32)
            for r in range(SUB if p >= q else 0):
                v = r_ref[SUB * q + r, eight(p), :]
                v = pltpu.roll(v, (r - offset) % WIDE, 1) if offset != r else v
                tile = jnp.where(cell == r, v, tile)
            columns.append(tile)
    return jnp.concatenate(columns, axis=0).T


def chol_kernel(*refs):
    *inputs, r_ref, a_ref, scale_ref = refs
    slots = [(ref, s) for ref in inputs for s in range(ref.shape[0] // RANK)]
    load_slots(slots, a_ref)
    chol_lanes(a_ref, r_ref, scale_ref)


def table_kernel(count, r_ref, left, right):
    keep = lane_half(2 * SUB)
    for q in range(0, NB, 2):
        for g in range(-(-count // CELL)):
            upper = factor_tiles(r_ref, q, g)
            lower = factor_tiles(r_ref, q + 1, g)
            for b in range(min(CELL, count - CELL * g)):
                both = jnp.concatenate([upper[eight(b)], lower[eight(b)]], axis=0)
                other = swapped(both)
                s = CELL * g + b
                for n, here, there in ((s, both, other), (count + s, other, both)):
                    at = n * WIDE + SUB * q
                    for table, value in (
                        (left, jnp.where(keep, here, 0.0)),
                        (right, jnp.where(keep, 0.0, there)),
                    ):
                        high, low = split(value)
                        table[at : at + 2 * SUB, :] = high
                        table[at + RANK : at + RANK + 2 * SUB, :] = low


def final_kernel(high, row_out, col_out, a_ref, r_ref, scale_ref):
    for i in range(RANK):
        b0 = SUB * (i // SUB)
        value = high[b0:RANK, :]
        a_ref[i, b0:RANK, :] = pltpu.roll(value, WIDE - i, 1) if i else value
    chol_lanes(a_ref, r_ref, scale_ref)
    lane = lax.broadcasted_iota(jnp.int32, (SUB, WIDE), 1) % RANK
    columns = []
    for q in range(NB):
        tile = jnp.zeros((SUB, WIDE), F32)
        for i in range(SUB * (q + 1)):
            value = r_ref[i, eight(q), :]
            tile = jnp.where(lane == i, pltpu.roll(value, i, 1) if i else value, tile)
        columns.append(tile)
    columns = jnp.concatenate(columns, axis=0)
    rows = jnp.concatenate([columns, columns], axis=0).T
    for out, half in ((row_out, rows[:RANK]), (col_out, rows[RANK:])):
        for k in range(RANK // 2):
            out[0, 0:1, lanes_of(k)] = beside(half[2 * k : 2 * k + 1], half[2 * k + 1 : 2 * k + 2])


def couple_kernel(
    first_group, groups, left_of, right_of, left_pick, right_pick, left, right, blocks, *refs
):
    target, s_ref, y_ref, out, sem = refs[-5:]

    def copy(g):
        at = pl.ds(pl.multiple_of(g * 2 * SUB, 2 * SUB), 2 * SUB)
        to = pl.ds(pl.multiple_of((first_group + g) * 2 * SUB, 2 * SUB), 2 * SUB)
        return pltpu.make_async_copy(out.at[at, :], target.at[0, to, :], sem.at[g])

    def group(g, carry):
        local = pl.multiple_of(g * 2 * SUB, 2 * SUB)
        start = pl.multiple_of((first_group + g) * 2 * SUB, 2 * SUB)

        def slab(k):
            return blocks[0, pl.ds(start, 2 * SUB), lanes_of(k)].astype(F32)

        def keep(b, q, tile):
            s_ref[b * RANK + SUB * q : b * RANK + SUB * (q + 1), :] = tile

        unpack_both(lambda k: slab(k)[:SUB], lambda k: slab(k)[SUB:], keep)

        def entry(table, pick, ref, b):
            return table[pl.ds(pl.multiple_of(pick(ref, start + b) * WIDE, WIDE), WIDE), :]

        for b in range(SUB):
            block = s_ref[b * RANK : (b + 1) * RANK, :].astype(BF16)
            rows = jnp.concatenate(
                [entry(left, left_of, left_pick, n)[:, :RANK] for n in (b, b + SUB)], axis=0
            )
            x = dot(rows, block)
            x = beside(x[:RANK], x[WIDE : WIDE + RANK]) + beside(
                x[RANK:WIDE], x[WIDE + RANK :]
            )
            first = entry(left, right_of, right_pick, b)
            second = entry(right, right_of, right_pick, b + SUB)
            weights = jnp.concatenate(
                [first[:RANK], second[:RANK], first[RANK:], second[RANK:]], axis=0
            )
            y = dot(stacked(x), weights, 1)
            y = y[:RANK] + y[RANK:]
            y_ref[b * RANK : (b + 1) * RANK, :] = y[:, :WIDE] + y[:, WIDE:]
        for q in range(NB):
            rows = swap8(
                [y_ref[b * RANK + SUB * q : b * RANK + SUB * (q + 1), :] for b in range(SUB)]
            )
            for k in range(SUB // 2):
                even, odd = rows[2 * k], rows[2 * k + 1]
                at = lanes_of(SUB // 2 * q + k)
                out[pl.ds(local, SUB), at] = beside(even, swapped(odd))
                out[pl.ds(pl.multiple_of(local + SUB, SUB), SUB), at] = beside(
                    swapped(even), odd
                )
        copy(g).start()
        return carry

    lax.fori_loop(0, groups, group, 0)
    for g in range(groups):
        copy(g).wait()


def shape(*dims):
    return jax.ShapeDtypeStruct(dims, F32)


def scratch(rows, lanes=WIDE):
    return pltpu.VMEM((rows, lanes), F32)


def call(kernel, outs, specs, scratches=(), limit=8):
    return pl.pallas_call(
        kernel,
        out_shape=outs,
        in_specs=specs,
        out_specs=jax.tree.map(lambda _: VMEM, outs),
        scratch_shapes=list(scratches),
        compiler_params=pltpu.CompilerParams(vmem_limit_bytes=limit << 20),
    )


def partner(value, axis, bit):
    return lax.ppermute(value, axis, [(i, i ^ 1 << bit) for i in range(lax.axis_size(axis))])


def body(
    row_bases,
    col_bases,
    row_transfer,
    col_transfer,
    row_order,
    col_order,
    leaf_pattern,
    leaf_blocks,
    root_rows,
    root_cols,
    root_blocks,
):
    count = row_bases.shape[1]
    nr, nc = lax.axis_size("row"), lax.axis_size("col")
    lr, lc = nr.bit_length() - 1, nc.bit_length() - 1
    top = lr + lc - 1

    leaf_gram, row_pay, col_pay, high, leaf_pattern, root_rows, root_cols = call(
        functools.partial(tree_kernel, count),
        [shape(count * RANK, WIDE), shape(WIDE, WIDE), shape(WIDE, WIDE), shape(RANK, WIDE)]
        + [jax.ShapeDtypeStruct(x.shape, x.dtype) for x in (leaf_pattern, root_rows, root_cols)],
        [HBM] * 9,
        [pltpu.VMEM(x.shape, F32) for x in (row_bases, col_bases, row_transfer, col_transfer)]
        + [pltpu.SMEM(x.shape, jnp.int32) for x in (row_order, col_order)]
        + [scratch(count * RANK), scratch(2 * count * RANK), pltpu.SemaphoreType.DMA((9,))],
    )(
        *(
            pltpu.with_memory_space_constraint(x, pltpu.HBM)
            for x in (
                row_order,
                col_order,
                row_bases,
                col_bases,
                row_transfer,
                col_transfer,
                leaf_pattern,
                root_rows,
                root_cols,
            )
        )
    )

    def step(levels, pay, axis, bit, high, held=0, apart=False, extra=None):
        recv = partner(pay, axis, bit)
        rows = sum(level < top for _, level in levels) * RANK
        rows += 0 if apart else held * RANK
        rows += 0 if extra is None else WIDE
        outs = [shape(RANK, WIDE)]
        if rows:
            outs.append(shape(rows, WIDE))
        if apart:
            outs.append(shape(held * RANK, WIDE))
        args = [pay, recv, high] + ([] if extra is None else [extra])
        result = call(
            functools.partial(step_kernel, levels, top, (nr, nc), held, apart, extra is not None),
            outs,
            [VMEM] * len(args),
            limit=2 + held // 4,
        )(*args)
        return result

    pay = col_pay
    for h in range(lr):
        done = h == lr - 1
        high, pay, *rest = step(
            [("c", h)],
            pay,
            "row",
            h,
            high,
            held=1 << h,
            apart=done,
            extra=row_pay if done else None,
        )
    col_roots = rest[0]
    for h in range(lc):
        done = h == lc - 1
        high, pay, *rest = step(
            [("r", h), ("c", lr + h)], pay, "col", h, high, held=1 << h, apart=done
        )
    row_roots = rest[0]
    for h in range(lr):
        high, *rest = step([("r", lc + h)], pay, "row", h, high)
        pay = rest[0] if rest else None

    big = [pltpu.VMEM((RANK, RANK, WIDE), F32)] * 2 + [pltpu.VMEM((RANK, SUB, WIDE), F32)]

    def tables(count, *sources):
        factors = call(
            chol_kernel, shape(RANK, RANK, WIDE), [VMEM] * len(sources), big[1:]
        )(*sources)
        out = jax.ShapeDtypeStruct((2 * count * WIDE, WIDE), BF16)
        return call(
            functools.partial(table_kernel, count), [out, out], [VMEM], limit=5 + count // 4
        )(factors)

    def couple(parts, left_of, right_of, left_pick, right_pick, factors, blocks):
        result, first = [], 0
        for groups in parts:
            pairs = groups * 2 * SUB
            result = [
                pl.pallas_call(
                    functools.partial(couple_kernel, first, groups, left_of, right_of),
                    out_shape=shape(1, blocks.shape[1], RANK * RANK),
                    in_specs=[SMEM, SMEM, VMEM, VMEM, VMEM] + [HBM] * len(result),
                    out_specs=HBM,
                    scratch_shapes=[
                        scratch(SUB * RANK),
                        scratch(SUB * RANK),
                        scratch(pairs, RANK * RANK),
                        pltpu.SemaphoreType.DMA((groups,)),
                    ],
                    input_output_aliases={5: 0} if result else {},
                    compiler_params=pltpu.CompilerParams(vmem_limit_bytes=6 << 20),
                )(left_pick, right_pick, *factors, blocks, *result)
            ]
            first += groups
        return result[0]

    leaf_groups = leaf_blocks.shape[1] // (2 * SUB)
    root_groups = root_blocks.shape[1] // (2 * SUB)
    leaf_coupled = couple(
        (leaf_groups // 2, leaf_groups - leaf_groups // 2),
        lambda ref, b: ref[0, 0, b],
        lambda ref, b: ref[0, 1, b] + count,
        leaf_pattern,
        leaf_pattern,
        tables(count, leaf_gram),
        leaf_blocks,
    )
    row_slots, col_slots = nc // 2, nr // 2
    slots = row_slots + col_slots
    root_coupled = couple(
        (root_groups,),
        lambda ref, b: (ref[0, 0, b] & 1) * slots + (ref[0, 0, b] >> 1),
        lambda ref, b: (ref[0, 0, b] & 1) * slots + (ref[0, 0, b] >> 1) + row_slots,
        root_rows,
        root_cols,
        tables(slots, row_roots, col_roots),
        root_blocks,
    )
    row_upper_r, col_upper_r = call(
        final_kernel, [shape(1, 1, RANK * RANK), shape(1, 1, RANK * RANK)], [VMEM], big
    )(high)
    return (leaf_coupled, root_coupled, row_upper_r, col_upper_r)


def solution(mesh):
    return jax.shard_map(
        body,
        mesh=mesh,
        in_specs=(
            P("row", "col", None),
            P("col", "row", None),
            P("row", "col", None),
            P("col", "row", None),
            P("row", "col", None),
            P("col", "row", None),
            P("row", "col", None),
            P("row", "col", None),
            P("row", "col", None),
            P("row", "col", None),
            P("row", "col", None),
        ),
        out_specs=(
            P("row", "col", None),
            P("row", "col", None),
            P("row", "col", None),
            P("col", "row", None),
        ),
        check_vma=False,
    )
```

```python
import functools

import jax
import jax.numpy as jnp
from jax import lax
from jax.experimental import pallas as pl
from jax.experimental.pallas import tpu as pltpu
from jax.sharding import PartitionSpec as P


RANK = 64
WIDE = 2 * RANK
SUB = 8
NB = RANK // SUB
F32 = jnp.float32
BF16 = jnp.bfloat16
VMEM = pl.BlockSpec(memory_space=pltpu.VMEM)
SMEM = pl.BlockSpec(memory_space=pltpu.SMEM)
HBM = pl.BlockSpec(memory_space=pltpu.HBM)


def split(x):
    high = x.astype(BF16)
    return high, (x - high.astype(F32)).astype(BF16)


def dot(a, b, rhs_dim=0):
    return lax.dot_general(a, b, (((1,), (rhs_dim,)), ((), ())), preferred_element_type=F32)


def dot3(a, b):
    a_high, a_low = split(a)
    b_high, b_low = split(b)
    return dot(a_high, b_high) + (dot(a_high, b_low) + dot(a_low, b_high))


def stacked(x, axis=0):
    return jnp.concatenate(split(x), axis=axis)


def lane_half(rows):
    return lax.broadcasted_iota(jnp.int32, (rows, WIDE), 1) < RANK


def swapped(x):
    return pltpu.roll(x, RANK, 1)


def beside(left, right):
    return jnp.where(lane_half(left.shape[0]), left, right)


def dot_both(a, b):
    y = dot(stacked(a), stacked(b))
    return beside(y[:RANK], y[RANK:WIDE]) + beside(y[WIDE : WIDE + RANK], y[WIDE + RANK :])


def sandwich_both(gram, transfer):
    x = dot(stacked(jnp.concatenate([transfer, transfer], axis=0).T), stacked(gram))
    x = x[:WIDE] + x[WIDE:]
    top, low = x[:RANK], x[RANK:]
    return dot_both(
        jnp.concatenate([beside(top, swapped(top)), beside(swapped(low), low)], axis=0), transfer
    )


def swap8(tiles):
    tiles = list(tiles)
    sub = lax.broadcasted_iota(jnp.int32, tiles[0].shape, 0)
    for d in (4, 2, 1):
        keep = (sub & d) == 0
        for i in range(SUB):
            if not i & d:
                a, b = tiles[i], tiles[i + d]
                tiles[i] = jnp.where(keep, a, pltpu.roll(b, d, 0))
                tiles[i + d] = jnp.where(keep, pltpu.roll(a, SUB - d, 0), b)
    return tiles


def eight(n):
    return slice(SUB * n, SUB * (n + 1))


def unpack_both(left, right, store):
    for q in range(NB):
        rows = []
        for k in range(SUB // 2 * q, SUB // 2 * (q + 1)):
            a, b = left(k), right(k)
            rows += [beside(a, swapped(b)), beside(swapped(a), b)]
        for b, tile in enumerate(swap8(rows)):
            store(b, q, tile)


def lanes_of(k):
    return slice(k * WIDE, (k + 1) * WIDE)


def unpack_trees(left_ref, right_ref, out_ref, count):
    for g in range(count // SUB):

        def store(b, q, tile):
            at = (SUB * g + b) * RANK + SUB * q
            out_ref[at : at + SUB, :] = tile

        unpack_both(
            lambda k: left_ref[0, eight(g), lanes_of(k)],
            lambda k: right_ref[0, eight(g), lanes_of(k)],
            store,
        )


def tree_kernel(
    count,
    row_order_in,
    col_order_in,
    row_bases_in,
    col_bases_in,
    row_transfer_in,
    col_transfer_in,
    *refs,
):
    picks_in, refs = refs[:3], refs[3:]
    leaf_gram, row_pay, col_pay, high = refs[:4]
    picks, refs = refs[4:7], refs[7:]
    (
        row_bases,
        col_bases,
        row_transfer,
        col_transfer,
        row_order,
        col_order,
        basis,
        trans,
        sems,
    ) = refs
    copies = [
        pltpu.make_async_copy(source, target, sems.at[n])
        for n, (source, target) in enumerate(
            (
                (row_bases_in, row_bases),
                (col_bases_in, col_bases),
                (row_transfer_in, row_transfer),
                (col_transfer_in, col_transfer),
                (row_order_in, row_order),
                (col_order_in, col_order),
                *zip(picks_in, picks),
            )
        )
    ]
    for copy in copies:
        copy.start()
    copies[0].wait()
    copies[1].wait()
    unpack_trees(row_bases, col_bases, basis, count)
    for leaf in range(count):
        u = basis[leaf * RANK : (leaf + 1) * RANK, :]
        leaf_gram[leaf * RANK : (leaf + 1) * RANK, :] = dot_both(
            jnp.concatenate([u, u], axis=0).T, u
        )
    for copy in copies[2:6]:
        copy.wait()
    unpack_trees(row_transfer, col_transfer, trans, 2 * count)
    nodes = []
    for q in range(count // 2):
        total = None
        for p in (2 * q, 2 * q + 1):
            r = pl.ds(pl.multiple_of(row_order[0, 0, p] * RANK, RANK), RANK)
            c = pl.ds(pl.multiple_of(col_order[0, 0, p] * RANK, RANK), RANK)
            term = sandwich_both(
                beside(leaf_gram[r, :], leaf_gram[c, :]), beside(trans[r, :], trans[c, :])
            )
            total = term if total is None else total + term
        nodes.append(total)
    offset = count
    while len(nodes) > 1:
        terms = []
        for q, gram in enumerate(nodes):
            terms.append(
                sandwich_both(gram, trans[(offset + q) * RANK : (offset + q + 1) * RANK, :])
            )
        offset += len(nodes)
        nodes = [terms[2 * q] + terms[2 * q + 1] for q in range(len(terms) // 2)]
    gram = nodes[0]
    term = sandwich_both(gram, trans[offset * RANK : (offset + 1) * RANK, :])
    first = trans[(offset + 1) * RANK : (offset + 2) * RANK, :]
    high[...] = gram
    row_pay[0:RANK, :] = beside(term, swapped(first))
    row_pay[RANK:WIDE, :] = gram
    col_pay[0:RANK, :] = beside(swapped(term), first)
    col_pay[RANK:WIDE, :] = swapped(gram)
    for copy in copies[6:]:
        copy.wait()


def step_kernel(levels, top, sizes, held, apart, extra, own, recv, high_in, *refs):
    refs = list(refs)
    before = refs.pop(0) if extra else None
    high_out = refs.pop(0)
    roots_out = refs.pop() if apart else None
    pay_out = refs.pop(0) if refs else None
    nr, nc = sizes
    i, j = lax.axis_index("row"), lax.axis_index("col")
    base = 0
    if extra:
        pay_out[0:RANK, :] = before[0:RANK, :]
        base = RANK
    high = high_in[...]
    uppers = []
    for slot, (name, level) in enumerate(levels):
        d = i * nc + j if name == "r" else j * nr + i
        span = 1 << level
        upper = lax.rem(lax.div(d, span), 2) == 1
        uppers.append(upper)
        take = lax.rem(d, 2 * span) == span
        if level == top:
            take = jnp.logical_or(take, d == 0)
        mine = own[slot * RANK : (slot + 1) * RANK, :]
        theirs = recv[slot * RANK : (slot + 1) * RANK, :]
        total = mine + theirs
        if level < top:
            transfer = jnp.where(upper, mine, theirs)
            first = jnp.where(upper, theirs, mine)
            x = dot3(transfer.T[RANK:], total[:, :RANK])
            pay_out[base : base + RANK, :] = beside(swapped(dot3(x, transfer)), first)
            base += RANK
        picked = beside(total, high) if name == "r" else beside(high, swapped(total))
        high = jnp.where(take, picked, high)
    high_out[...] = high
    if extra:
        pay_out[base : base + RANK, :] = before[RANK:WIDE, :]
    if held:
        upper = uppers[0]
        start = len(levels) * RANK
        if roots_out is None:
            roots_out = pay_out.at[base:, :]
        if held == 1:
            mine = own[start : start + RANK, :]
            theirs = recv[start : start + RANK, :]
            roots_out[0:RANK, :] = jnp.where(
                upper, beside(theirs, swapped(mine)), beside(mine, swapped(theirs))
            )
        else:
            rows = held // 2 * RANK
            mine = own[start : start + rows, :]
            theirs = recv[start : start + rows, :]
            roots_out[0:rows, :] = jnp.where(upper, theirs, mine)
            roots_out[rows : 2 * rows, :] = jnp.where(upper, mine, theirs)


def chol_lanes(a_ref, r_ref, scale_ref, begin=-1, end=NB - 1):
    sub = lax.broadcasted_iota(jnp.int32, (SUB, WIDE), 0)
    here = lax.axis_index("row") >= 0

    def spread(i, j):
        return r_ref[i, pl.ds(j, SUB, stride=0), :]

    def less(value, f, row):
        return lax.sub(value, lax.mul(f, row))

    def reduced(p, qs):
        acc = {(r, q): a_ref[SUB * p + r, eight(q), :] for r in range(SUB) for q in qs}
        for k in range(SUB * p):
            rows = [r_ref[k, eight(q), :] for q in qs]
            for r in range(SUB):
                f = spread(k, SUB * p + r)
                for q, row in zip(qs, rows):
                    acc[r, q] = less(acc[r, q], f, row)
        return acc

    def diagonal(p):
        acc = reduced(p, [p])
        for r in range(SUB):
            inv = lax.rsqrt(jnp.broadcast_to(acc[r, p][r : r + 1, :], (SUB, WIDE)))
            scale_ref[SUB * p + r] = inv
            row = jnp.where(sub >= r, lax.mul(acc[r, p], inv), 0.0)
            r_ref[SUB * p + r, eight(p), :] = row
            for r2 in range(r + 1, SUB):
                f = jnp.broadcast_to(row[r2 : r2 + 1, :], (SUB, WIDE))
                acc[r2, p] = less(acc[r2, p], f, row)

    def beyond(p, qs):
        acc = reduced(p, qs)
        for r in range(SUB):
            inv = scale_ref[SUB * p + r]
            for q in qs:
                acc[r, q] = lax.mul(acc[r, q], inv)
                r_ref[SUB * p + r, eight(q), :] = acc[r, q]
            for r2 in range(r + 1, SUB):
                f = spread(SUB * p + r, SUB * p + r2)
                for q in qs:
                    acc[r2, q] = less(acc[r2, q], f, acc[r, q])

    for p in range(begin, end):

        @pl.when(here)
        def _():
            if p >= 0:
                beyond(p, [p + 1])
            diagonal(p + 1)
            for q in range(p + 2, NB, 2):
                if p >= 0:
                    beyond(p, list(range(q, min(q + 2, NB))))


CELL = WIDE // SUB
CUT = NB // 2


def load_slots(slots, a_ref):
    cell = lax.broadcasted_iota(jnp.int32, (RANK, WIDE), 1) % SUB
    for q in range(NB):
        b0 = SUB * q
        turned = []
        for g in range(0, len(slots), CELL):
            group = slots[g : g + CELL]
            group = group + [group[-1]] * (CELL - len(group))
            tiles = [ref[s * RANK + b0 : s * RANK + b0 + SUB, :] for ref, s in group]
            t = jnp.concatenate(tiles, axis=0).T
            turned += [t[b0:RANK], t[RANK + b0 :]]
        for r in range(SUB):
            value = None
            for offset, t in enumerate(turned):
                t = pltpu.roll(t, (offset - r) % WIDE, 1) if offset != r else t
                value = t if value is None else jnp.where(cell[b0:] == offset, t, value)
            a_ref[b0 + r, b0:RANK, :] = value


def factor_tiles(r_ref, q, group):
    cell = lax.broadcasted_iota(jnp.int32, (SUB, WIDE), 1) % SUB
    columns = []
    for half in range(2):
        offset = 2 * group + half
        for p in range(NB):
            tile = jnp.zeros((SUB, WIDE), F32)
            for r in range(SUB if p >= q else 0):
                v = r_ref[SUB * q + r, eight(p), :]
                v = pltpu.roll(v, (r - offset) % WIDE, 1) if offset != r else v
                tile = jnp.where(cell == r, v, tile)
            columns.append(tile)
    return jnp.concatenate(columns, axis=0).T


def chol_kernel(*refs):
    *inputs, r_ref, a_ref, scale_ref = refs
    slots = [(ref, s) for ref in inputs for s in range(ref.shape[0] // RANK)]
    load_slots(slots, a_ref)
    chol_lanes(a_ref, r_ref, scale_ref)


def chol_first_kernel(gram, r_ref, a_ref, scale_ref):
    slots = [(gram, s) for s in range(gram.shape[0] // RANK)]
    load_slots(slots, a_ref)
    chol_lanes(a_ref, r_ref, scale_ref, -1, CUT)


def chol_second_kernel(count, r_in, a_ref, scale_in, left, right, r_ref, scale_ref):
    for k in range(SUB * (CUT + 1)):
        last = CUT + 1 if k >= SUB * CUT else NB
        at = slice(SUB * (k // SUB), SUB * last)
        r_ref[k, at, :] = r_in[k, at, :]
    for k in range(SUB * CUT, SUB * (CUT + 1)):
        scale_ref[k] = scale_in[k]
    chol_lanes(a_ref, r_ref, scale_ref, CUT, NB - 1)
    table_kernel(count, r_ref, left, right)


def table_kernel(count, r_ref, left, right):
    keep = lane_half(2 * SUB)
    for q in range(0, NB, 2):
        for g in range(-(-count // CELL)):
            upper = factor_tiles(r_ref, q, g)
            lower = factor_tiles(r_ref, q + 1, g)
            for b in range(min(CELL, count - CELL * g)):
                both = jnp.concatenate([upper[eight(b)], lower[eight(b)]], axis=0)
                other = swapped(both)
                s = CELL * g + b
                for n, here, there in ((s, both, other), (count + s, other, both)):
                    at = n * WIDE + SUB * q
                    for table, value in (
                        (left, jnp.where(keep, here, 0.0)),
                        (right, jnp.where(keep, 0.0, there)),
                    ):
                        high, low = split(value)
                        table[at : at + 2 * SUB, :] = high
                        table[at + RANK : at + RANK + 2 * SUB, :] = low


def final_kernel(high, row_out, col_out, a_ref, r_ref, scale_ref):
    for i in range(RANK):
        b0 = SUB * (i // SUB)
        value = high[b0:RANK, :]
        a_ref[i, b0:RANK, :] = pltpu.roll(value, WIDE - i, 1) if i else value
    chol_lanes(a_ref, r_ref, scale_ref)
    lane = lax.broadcasted_iota(jnp.int32, (SUB, WIDE), 1) % RANK
    columns = []
    for q in range(NB):
        tile = jnp.zeros((SUB, WIDE), F32)
        for i in range(SUB * (q + 1)):
            value = r_ref[i, eight(q), :]
            tile = jnp.where(lane == i, pltpu.roll(value, i, 1) if i else value, tile)
        columns.append(tile)
    columns = jnp.concatenate(columns, axis=0)
    rows = jnp.concatenate([columns, columns], axis=0).T
    for out, half in ((row_out, rows[:RANK]), (col_out, rows[RANK:])):
        for k in range(RANK // 2):
            out[0, 0:1, lanes_of(k)] = beside(half[2 * k : 2 * k + 1], half[2 * k + 1 : 2 * k + 2])


def couple_kernel(
    first_group, groups, left_of, right_of, left_pick, right_pick, left, right, blocks, *refs
):
    target, s_ref, y_ref, out, sem = refs[-5:]

    def copy(g):
        at = pl.ds(pl.multiple_of(g * 2 * SUB, 2 * SUB), 2 * SUB)
        to = pl.ds(pl.multiple_of((first_group + g) * 2 * SUB, 2 * SUB), 2 * SUB)
        return pltpu.make_async_copy(out.at[at, :], target.at[0, to, :], sem.at[g])

    def group(g, s_ref, y_ref):
        local = pl.multiple_of(g * 2 * SUB, 2 * SUB)
        start = pl.multiple_of((first_group + g) * 2 * SUB, 2 * SUB)

        def slab(k):
            return blocks[0, pl.ds(start, 2 * SUB), lanes_of(k)].astype(F32)

        def keep(b, q, tile):
            s_ref[b * RANK + SUB * q : b * RANK + SUB * (q + 1), :] = tile

        unpack_both(lambda k: slab(k)[:SUB], lambda k: slab(k)[SUB:], keep)

        def entry(table, pick, ref, b):
            return table[pl.ds(pl.multiple_of(pick(ref, start + b) * WIDE, WIDE), WIDE), :]

        for b in range(SUB):
            block = s_ref[b * RANK : (b + 1) * RANK, :].astype(BF16)
            rows = jnp.concatenate(
                [entry(left, left_of, left_pick, n)[:, :RANK] for n in (b, b + SUB)], axis=0
            )
            x = dot(rows, block)
            x = beside(x[:RANK], x[WIDE : WIDE + RANK]) + beside(
                x[RANK:WIDE], x[WIDE + RANK :]
            )
            first = entry(left, right_of, right_pick, b)
            second = entry(right, right_of, right_pick, b + SUB)
            weights = jnp.concatenate(
                [first[:RANK], second[:RANK], first[RANK:], second[RANK:]], axis=0
            )
            y = dot(stacked(x), weights, 1)
            y = y[:RANK] + y[RANK:]
            y_ref[b * RANK : (b + 1) * RANK, :] = y[:, :WIDE] + y[:, WIDE:]
        for q in range(NB):
            rows = swap8(
                [y_ref[b * RANK + SUB * q : b * RANK + SUB * (q + 1), :] for b in range(SUB)]
            )
            for k in range(SUB // 2):
                even, odd = rows[2 * k], rows[2 * k + 1]
                at = lanes_of(SUB // 2 * q + k)
                out[pl.ds(local, SUB), at] = beside(even, swapped(odd))
                out[pl.ds(pl.multiple_of(local + SUB, SUB), SUB), at] = beside(
                    swapped(even), odd
                )
        copy(g).start()

    for g in range(groups):
        group(g, s_ref.at[g % 2], y_ref.at[g % 2])
    for g in range(groups):
        copy(g).wait()


def shape(*dims):
    return jax.ShapeDtypeStruct(dims, F32)


def scratch(rows, lanes=WIDE):
    return pltpu.VMEM((rows, lanes), F32)


def call(kernel, outs, specs, scratches=(), limit=8):
    return pl.pallas_call(
        kernel,
        out_shape=outs,
        in_specs=specs,
        out_specs=jax.tree.map(lambda _: VMEM, outs),
        scratch_shapes=list(scratches),
        compiler_params=pltpu.CompilerParams(vmem_limit_bytes=limit << 20),
    )


def partner(value, axis, bit):
    return lax.ppermute(value, axis, [(i, i ^ 1 << bit) for i in range(lax.axis_size(axis))])


def body(
    row_bases,
    col_bases,
    row_transfer,
    col_transfer,
    row_order,
    col_order,
    leaf_pattern,
    leaf_blocks,
    root_rows,
    root_cols,
    root_blocks,
):
    count = row_bases.shape[1]
    nr, nc = lax.axis_size("row"), lax.axis_size("col")
    lr, lc = nr.bit_length() - 1, nc.bit_length() - 1
    top = lr + lc - 1

    leaf_gram, row_pay, col_pay, high, leaf_pattern, root_rows, root_cols = call(
        functools.partial(tree_kernel, count),
        [shape(count * RANK, WIDE), shape(WIDE, WIDE), shape(WIDE, WIDE), shape(RANK, WIDE)]
        + [jax.ShapeDtypeStruct(x.shape, x.dtype) for x in (leaf_pattern, root_rows, root_cols)],
        [HBM] * 9,
        [pltpu.VMEM(x.shape, F32) for x in (row_bases, col_bases, row_transfer, col_transfer)]
        + [pltpu.SMEM(x.shape, jnp.int32) for x in (row_order, col_order)]
        + [scratch(count * RANK), scratch(2 * count * RANK), pltpu.SemaphoreType.DMA((9,))],
    )(
        *(
            pltpu.with_memory_space_constraint(x, pltpu.HBM)
            for x in (
                row_order,
                col_order,
                row_bases,
                col_bases,
                row_transfer,
                col_transfer,
                leaf_pattern,
                root_rows,
                root_cols,
            )
        )
    )

    def step(levels, pay, axis, bit, high, held=0, apart=False, extra=None):
        recv = partner(pay, axis, bit)
        rows = sum(level < top for _, level in levels) * RANK
        rows += 0 if apart else held * RANK
        rows += 0 if extra is None else WIDE
        outs = [shape(RANK, WIDE)]
        if rows:
            outs.append(shape(rows, WIDE))
        if apart:
            outs.append(shape(held * RANK, WIDE))
        args = [pay, recv, high] + ([] if extra is None else [extra])
        result = call(
            functools.partial(step_kernel, levels, top, (nr, nc), held, apart, extra is not None),
            outs,
            [VMEM] * len(args),
            limit=2 + held // 4,
        )(*args)
        return result

    pay = col_pay
    for h in range(lr):
        done = h == lr - 1
        high, pay, *rest = step(
            [("c", h)],
            pay,
            "row",
            h,
            high,
            held=1 << h,
            apart=done,
            extra=row_pay if done else None,
        )
    col_roots = rest[0]
    for h in range(lc):
        done = h == lc - 1
        high, pay, *rest = step(
            [("r", h), ("c", lr + h)], pay, "col", h, high, held=1 << h, apart=done
        )
    row_roots = rest[0]
    for h in range(lr):
        high, *rest = step([("r", lc + h)], pay, "row", h, high)
        pay = rest[0] if rest else None

    big = [pltpu.VMEM((RANK, RANK, WIDE), F32)] * 2 + [pltpu.VMEM((RANK, SUB, WIDE), F32)]

    def leaf_tables(count, gram):
        parts = call(
            chol_first_kernel,
            [
                shape(RANK, RANK, WIDE),
                shape(RANK, RANK, WIDE),
                shape(RANK, SUB, WIDE),
            ],
            [VMEM],
        )(gram)
        out = jax.ShapeDtypeStruct((2 * count * WIDE, WIDE), BF16)
        return call(
            functools.partial(chol_second_kernel, count), [out, out], [VMEM] * 3, big[1:], limit=12
        )(*parts)

    def root_tables(count, *sources):
        factors = call(
            chol_kernel, shape(RANK, RANK, WIDE), [VMEM] * len(sources), big[1:]
        )(*sources)
        out = jax.ShapeDtypeStruct((2 * count * WIDE, WIDE), BF16)
        return call(
            functools.partial(table_kernel, count), [out, out], [VMEM], limit=5 + count // 4
        )(factors)

    def couple(parts, left_of, right_of, left_pick, right_pick, factors, blocks):
        result, first = [], 0
        for groups in parts:
            pairs = groups * 2 * SUB
            result = [
                pl.pallas_call(
                    functools.partial(couple_kernel, first, groups, left_of, right_of),
                    out_shape=shape(1, blocks.shape[1], RANK * RANK),
                    in_specs=[SMEM, SMEM, VMEM, VMEM, VMEM] + [HBM] * len(result),
                    out_specs=HBM,
                    scratch_shapes=[
                        pltpu.VMEM((2, SUB * RANK, WIDE), F32),
                        pltpu.VMEM((2, SUB * RANK, WIDE), F32),
                        scratch(pairs, RANK * RANK),
                        pltpu.SemaphoreType.DMA((groups,)),
                    ],
                    input_output_aliases={5: 0} if result else {},
                    compiler_params=pltpu.CompilerParams(vmem_limit_bytes=6 << 20),
                )(left_pick, right_pick, *factors, blocks, *result)
            ]
            first += groups
        return result[0]

    leaf_groups = leaf_blocks.shape[1] // (2 * SUB)
    root_groups = root_blocks.shape[1] // (2 * SUB)
    leaf_coupled = couple(
        (leaf_groups // 2, leaf_groups - leaf_groups // 2),
        lambda ref, b: ref[0, 0, b],
        lambda ref, b: ref[0, 1, b] + count,
        leaf_pattern,
        leaf_pattern,
        leaf_tables(count, leaf_gram),
        leaf_blocks,
    )
    row_slots, col_slots = nc // 2, nr // 2
    slots = row_slots + col_slots
    root_coupled = couple(
        (root_groups,),
        lambda ref, b: (ref[0, 0, b] & 1) * slots + (ref[0, 0, b] >> 1),
        lambda ref, b: (ref[0, 0, b] & 1) * slots + (ref[0, 0, b] >> 1) + row_slots,
        root_rows,
        root_cols,
        root_tables(slots, row_roots, col_roots),
        root_blocks,
    )
    row_upper_r, col_upper_r = call(
        final_kernel, [shape(1, 1, RANK * RANK), shape(1, 1, RANK * RANK)], [VMEM], big
    )(high)
    return (leaf_coupled, root_coupled, row_upper_r, col_upper_r)


def solution(mesh):
    return jax.shard_map(
        body,
        mesh=mesh,
        in_specs=(
            P("row", "col", None),
            P("col", "row", None),
            P("row", "col", None),
            P("col", "row", None),
            P("row", "col", None),
            P("col", "row", None),
            P("row", "col", None),
            P("row", "col", None),
            P("row", "col", None),
            P("row", "col", None),
            P("row", "col", None),
        ),
        out_specs=(
            P("row", "col", None),
            P("row", "col", None),
            P("row", "col", None),
            P("col", "row", None),
        ),
        check_vma=False,
    )
```

```python
import functools

import jax
import jax.numpy as jnp
from jax import lax
from jax.experimental import pallas as pl
from jax.experimental.pallas import tpu as pltpu
from jax.sharding import PartitionSpec as P


RANK = 64
WIDE = 2 * RANK
SUB = 8
NB = RANK // SUB
F32 = jnp.float32
BF16 = jnp.bfloat16
VMEM = pl.BlockSpec(memory_space=pltpu.VMEM)
SMEM = pl.BlockSpec(memory_space=pltpu.SMEM)
HBM = pl.BlockSpec(memory_space=pltpu.HBM)


def split(x):
    high = x.astype(BF16)
    return high, (x - high.astype(F32)).astype(BF16)


def dot(a, b, rhs_dim=0):
    return lax.dot_general(a, b, (((1,), (rhs_dim,)), ((), ())), preferred_element_type=F32)


def dot3(a, b):
    a_high, a_low = split(a)
    b_high, b_low = split(b)
    return dot(a_high, b_high) + (dot(a_high, b_low) + dot(a_low, b_high))


def stacked(x, axis=0):
    return jnp.concatenate(split(x), axis=axis)


def lane_half(rows):
    return lax.broadcasted_iota(jnp.int32, (rows, WIDE), 1) < RANK


def swapped(x):
    return pltpu.roll(x, RANK, 1)


def beside(left, right):
    return jnp.where(lane_half(left.shape[0]), left, right)


def dot_both(a, b):
    y = dot(stacked(a), stacked(b))
    return beside(y[:RANK], y[RANK:WIDE]) + beside(y[WIDE : WIDE + RANK], y[WIDE + RANK :])


def sandwich_both(gram, transfer):
    x = dot(stacked(jnp.concatenate([transfer, transfer], axis=0).T), stacked(gram))
    x = x[:WIDE] + x[WIDE:]
    top, low = x[:RANK], x[RANK:]
    return dot_both(
        jnp.concatenate([beside(top, swapped(top)), beside(swapped(low), low)], axis=0), transfer
    )


def swap8(tiles):
    tiles = list(tiles)
    sub = lax.broadcasted_iota(jnp.int32, tiles[0].shape, 0)
    for d in (4, 2, 1):
        keep = (sub & d) == 0
        for i in range(SUB):
            if not i & d:
                a, b = tiles[i], tiles[i + d]
                tiles[i] = jnp.where(keep, a, pltpu.roll(b, d, 0))
                tiles[i + d] = jnp.where(keep, pltpu.roll(a, SUB - d, 0), b)
    return tiles


def eight(n):
    return slice(SUB * n, SUB * (n + 1))


def unpack_both(left, right, store):
    for q in range(NB):
        rows = []
        for k in range(SUB // 2 * q, SUB // 2 * (q + 1)):
            a, b = left(k), right(k)
            rows += [beside(a, swapped(b)), beside(swapped(a), b)]
        for b, tile in enumerate(swap8(rows)):
            store(b, q, tile)


def lanes_of(k):
    return slice(k * WIDE, (k + 1) * WIDE)


def unpack_trees(left_ref, right_ref, out_ref, count):
    for g in range(count // SUB):

        def store(b, q, tile):
            at = (SUB * g + b) * RANK + SUB * q
            out_ref[at : at + SUB, :] = tile

        unpack_both(
            lambda k: left_ref[0, eight(g), lanes_of(k)],
            lambda k: right_ref[0, eight(g), lanes_of(k)],
            store,
        )


def tree_kernel(
    count,
    row_order_in,
    col_order_in,
    row_bases_in,
    col_bases_in,
    row_transfer_in,
    col_transfer_in,
    *refs,
):
    picks_in, refs = refs[:3], refs[3:]
    leaf_gram, row_pay, col_pay, high = refs[:4]
    picks, refs = refs[4:7], refs[7:]
    (
        row_bases,
        col_bases,
        row_transfer,
        col_transfer,
        row_order,
        col_order,
        basis,
        trans,
        sems,
    ) = refs
    copies = [
        pltpu.make_async_copy(source, target, sems.at[n])
        for n, (source, target) in enumerate(
            (
                (row_bases_in, row_bases),
                (col_bases_in, col_bases),
                (row_transfer_in, row_transfer),
                (col_transfer_in, col_transfer),
                (row_order_in, row_order),
                (col_order_in, col_order),
                *zip(picks_in, picks),
            )
        )
    ]
    for copy in copies:
        copy.start()
    copies[0].wait()
    copies[1].wait()
    unpack_trees(row_bases, col_bases, basis, count)
    for leaf in range(count):
        u = basis[leaf * RANK : (leaf + 1) * RANK, :]
        leaf_gram[leaf * RANK : (leaf + 1) * RANK, :] = dot_both(
            jnp.concatenate([u, u], axis=0).T, u
        )
    for copy in copies[2:6]:
        copy.wait()
    unpack_trees(row_transfer, col_transfer, trans, 2 * count)
    nodes = []
    for q in range(count // 2):
        total = None
        for p in (2 * q, 2 * q + 1):
            r = pl.ds(pl.multiple_of(row_order[0, 0, p] * RANK, RANK), RANK)
            c = pl.ds(pl.multiple_of(col_order[0, 0, p] * RANK, RANK), RANK)
            term = sandwich_both(
                beside(leaf_gram[r, :], leaf_gram[c, :]), beside(trans[r, :], trans[c, :])
            )
            total = term if total is None else total + term
        nodes.append(total)
    offset = count
    while len(nodes) > 1:
        terms = []
        for q, gram in enumerate(nodes):
            terms.append(
                sandwich_both(gram, trans[(offset + q) * RANK : (offset + q + 1) * RANK, :])
            )
        offset += len(nodes)
        nodes = [terms[2 * q] + terms[2 * q + 1] for q in range(len(terms) // 2)]
    gram = nodes[0]
    term = sandwich_both(gram, trans[offset * RANK : (offset + 1) * RANK, :])
    first = trans[(offset + 1) * RANK : (offset + 2) * RANK, :]
    high[...] = gram
    row_pay[0:RANK, :] = beside(term, swapped(first))
    row_pay[RANK:WIDE, :] = gram
    col_pay[0:RANK, :] = beside(swapped(term), first)
    col_pay[RANK:WIDE, :] = swapped(gram)
    for copy in copies[6:]:
        copy.wait()


def step_kernel(levels, top, sizes, held, apart, extra, own, recv, high_in, *refs):
    refs = list(refs)
    before = refs.pop(0) if extra else None
    high_out = refs.pop(0)
    roots_out = refs.pop() if apart else None
    pay_out = refs.pop(0) if refs else None
    nr, nc = sizes
    i, j = lax.axis_index("row"), lax.axis_index("col")
    base = 0
    if extra:
        pay_out[0:RANK, :] = before[0:RANK, :]
        base = RANK
    high = high_in[...]
    uppers = []
    for slot, (name, level) in enumerate(levels):
        d = i * nc + j if name == "r" else j * nr + i
        span = 1 << level
        upper = lax.rem(lax.div(d, span), 2) == 1
        uppers.append(upper)
        take = lax.rem(d, 2 * span) == span
        if level == top:
            take = jnp.logical_or(take, d == 0)
        mine = own[slot * RANK : (slot + 1) * RANK, :]
        theirs = recv[slot * RANK : (slot + 1) * RANK, :]
        total = mine + theirs
        if level < top:
            transfer = jnp.where(upper, mine, theirs)
            first = jnp.where(upper, theirs, mine)
            x = dot3(transfer.T[RANK:], total[:, :RANK])
            pay_out[base : base + RANK, :] = beside(swapped(dot3(x, transfer)), first)
            base += RANK
        picked = beside(total, high) if name == "r" else beside(high, swapped(total))
        high = jnp.where(take, picked, high)
    high_out[...] = high
    if extra:
        pay_out[base : base + RANK, :] = before[RANK:WIDE, :]
    if held:
        upper = uppers[0]
        start = len(levels) * RANK
        if roots_out is None:
            roots_out = pay_out.at[base:, :]
        if held == 1:
            mine = own[start : start + RANK, :]
            theirs = recv[start : start + RANK, :]
            roots_out[0:RANK, :] = jnp.where(
                upper, beside(theirs, swapped(mine)), beside(mine, swapped(theirs))
            )
        else:
            rows = held // 2 * RANK
            mine = own[start : start + rows, :]
            theirs = recv[start : start + rows, :]
            roots_out[0:rows, :] = jnp.where(upper, theirs, mine)
            roots_out[rows : 2 * rows, :] = jnp.where(upper, mine, theirs)


def chol_lanes(a_ref, r_ref, scale_ref, begin=-1, end=NB - 1):
    sub = lax.broadcasted_iota(jnp.int32, (SUB, WIDE), 0)
    here = lax.axis_index("row") >= 0

    def spread(i, j):
        return r_ref[i, pl.ds(j, SUB, stride=0), :]

    def less(value, f, row):
        return lax.sub(value, lax.mul(f, row))

    def reduced(p, qs):
        acc = {(r, q): a_ref[SUB * p + r, eight(q), :] for r in range(SUB) for q in qs}
        for k in range(SUB * p):
            rows = [r_ref[k, eight(q), :] for q in qs]
            for r in range(SUB):
                f = spread(k, SUB * p + r)
                for q, row in zip(qs, rows):
                    acc[r, q] = less(acc[r, q], f, row)
        return acc

    def diagonal(p):
        acc = reduced(p, [p])
        for r in range(SUB):
            inv = lax.rsqrt(jnp.broadcast_to(acc[r, p][r : r + 1, :], (SUB, WIDE)))
            scale_ref[SUB * p + r] = inv
            row = jnp.where(sub >= r, lax.mul(acc[r, p], inv), 0.0)
            r_ref[SUB * p + r, eight(p), :] = row
            for r2 in range(r + 1, SUB):
                f = jnp.broadcast_to(row[r2 : r2 + 1, :], (SUB, WIDE))
                acc[r2, p] = less(acc[r2, p], f, row)

    def beyond(p, qs):
        acc = reduced(p, qs)
        for r in range(SUB):
            inv = scale_ref[SUB * p + r]
            for q in qs:
                acc[r, q] = lax.mul(acc[r, q], inv)
                r_ref[SUB * p + r, eight(q), :] = acc[r, q]
            for r2 in range(r + 1, SUB):
                f = spread(SUB * p + r, SUB * p + r2)
                for q in qs:
                    acc[r2, q] = less(acc[r2, q], f, acc[r, q])

    for p in range(begin, end):

        @pl.when(here)
        def _():
            if p >= 0:
                beyond(p, [p + 1])
            diagonal(p + 1)
            for q in range(p + 2, NB, 2):
                if p >= 0:
                    beyond(p, list(range(q, min(q + 2, NB))))


CELL = WIDE // SUB
CUT = NB // 2


def load_slots(slots, a_ref):
    cell = lax.broadcasted_iota(jnp.int32, (RANK, WIDE), 1) % SUB
    for q in range(NB):
        b0 = SUB * q
        if len(slots) <= SUB:
            group = slots + [slots[-1]] * (SUB - len(slots))
            tiles = [ref[s * RANK + b0 : s * RANK + b0 + SUB, :] for ref, s in group]
            t = jnp.concatenate(tiles, axis=0).T
            value = jnp.concatenate([t[b0:RANK], t[RANK + b0 :]], axis=1)
            for r in range(SUB):
                a_ref[b0 + r, b0:RANK, :] = pltpu.roll(value, WIDE - r, 1) if r else value
            continue
        turned = []
        for g in range(0, len(slots), CELL):
            group = slots[g : g + CELL]
            group = group + [group[-1]] * (CELL - len(group))
            tiles = [ref[s * RANK + b0 : s * RANK + b0 + SUB, :] for ref, s in group]
            t = jnp.concatenate(tiles, axis=0).T
            turned += [t[b0:RANK], t[RANK + b0 :]]
        for r in range(SUB):
            value = None
            for offset, t in enumerate(turned):
                t = pltpu.roll(t, (offset - r) % WIDE, 1) if offset != r else t
                value = t if value is None else jnp.where(cell[b0:] == offset, t, value)
            a_ref[b0 + r, b0:RANK, :] = value


def factor_tiles(r_ref, q, group):
    cell = lax.broadcasted_iota(jnp.int32, (SUB, WIDE), 1) % SUB
    columns = []
    for half in range(2):
        offset = 0 if group is None else 2 * group + half
        if group is None and half:
            columns += columns
            break
        for p in range(NB):
            tile = jnp.zeros((SUB, WIDE), F32)
            for r in range(SUB if p >= q else 0):
                v = r_ref[SUB * q + r, eight(p), :]
                v = pltpu.roll(v, (r - offset) % WIDE, 1) if offset != r else v
                tile = jnp.where(cell == r, v, tile)
            columns.append(tile)
    return jnp.concatenate(columns, axis=0).T


def chol_kernel(*refs):
    *inputs, r_ref, a_ref, scale_ref = refs
    slots = [(ref, s) for ref in inputs for s in range(ref.shape[0] // RANK)]
    load_slots(slots, a_ref)
    chol_lanes(a_ref, r_ref, scale_ref)


def chol_first_kernel(gram, r_ref, a_ref, scale_ref):
    slots = [(gram, s) for s in range(gram.shape[0] // RANK)]
    load_slots(slots, a_ref)
    chol_lanes(a_ref, r_ref, scale_ref, -1, CUT)


def chol_second_kernel(count, r_in, a_ref, scale_in, left, right, r_ref, scale_ref):
    for k in range(SUB * (CUT + 1)):
        last = CUT + 1 if k >= SUB * CUT else NB
        at = slice(SUB * (k // SUB), SUB * last)
        r_ref[k, at, :] = r_in[k, at, :]
    for k in range(SUB * CUT, SUB * (CUT + 1)):
        scale_ref[k] = scale_in[k]
    chol_lanes(a_ref, r_ref, scale_ref, CUT, NB - 1)
    table_kernel(count, r_ref, left, right)


def table_kernel(count, r_ref, left, right):
    keep = lane_half(2 * SUB)
    for q in range(0, NB, 2):
        if count <= SUB:
            upper = factor_tiles(r_ref, q, None)
            lower = factor_tiles(r_ref, q + 1, None)
            for half in range(2):
                for s in range(count):
                    rows = eight(SUB * half + s)
                    both = jnp.concatenate([upper[rows], lower[rows]], axis=0)
                    at = (half * count + s) * WIDE + SUB * q
                    for table, value in (
                        (left, jnp.where(keep, both, 0.0)),
                        (right, jnp.where(keep, 0.0, both)),
                    ):
                        high, low = split(value)
                        table[at : at + 2 * SUB, :] = high
                        table[at + RANK : at + RANK + 2 * SUB, :] = low
            continue
        for g in range(-(-count // CELL)):
            upper = factor_tiles(r_ref, q, g)
            lower = factor_tiles(r_ref, q + 1, g)
            for b in range(min(CELL, count - CELL * g)):
                both = jnp.concatenate([upper[eight(b)], lower[eight(b)]], axis=0)
                other = swapped(both)
                s = CELL * g + b
                for n, here, there in ((s, both, other), (count + s, other, both)):
                    at = n * WIDE + SUB * q
                    for table, value in (
                        (left, jnp.where(keep, here, 0.0)),
                        (right, jnp.where(keep, 0.0, there)),
                    ):
                        high, low = split(value)
                        table[at : at + 2 * SUB, :] = high
                        table[at + RANK : at + RANK + 2 * SUB, :] = low


def final_kernel(high, row_out, col_out, a_ref, r_ref, scale_ref):
    for i in range(RANK):
        b0 = SUB * (i // SUB)
        value = high[b0:RANK, :]
        a_ref[i, b0:RANK, :] = pltpu.roll(value, WIDE - i, 1) if i else value
    chol_lanes(a_ref, r_ref, scale_ref)
    lane = lax.broadcasted_iota(jnp.int32, (SUB, WIDE), 1) % RANK
    columns = []
    for q in range(NB):
        tile = jnp.zeros((SUB, WIDE), F32)
        for i in range(SUB * (q + 1)):
            value = r_ref[i, eight(q), :]
            tile = jnp.where(lane == i, pltpu.roll(value, i, 1) if i else value, tile)
        columns.append(tile)
    columns = jnp.concatenate(columns, axis=0)
    rows = jnp.concatenate([columns, columns], axis=0).T
    for out, half in ((row_out, rows[:RANK]), (col_out, rows[RANK:])):
        for k in range(RANK // 2):
            out[0, 0:1, lanes_of(k)] = beside(half[2 * k : 2 * k + 1], half[2 * k + 1 : 2 * k + 2])


def couple_kernel(
    first_group, groups, left_of, right_of, left_pick, right_pick, left, right, blocks, *refs
):
    target, s_ref, y_ref, out, sem = refs[-5:]

    def copy(g):
        at = pl.ds(pl.multiple_of(g * 2 * SUB, 2 * SUB), 2 * SUB)
        to = pl.ds(pl.multiple_of((first_group + g) * 2 * SUB, 2 * SUB), 2 * SUB)
        return pltpu.make_async_copy(out.at[at, :], target.at[0, to, :], sem.at[g])

    def group(g, s_ref, y_ref):
        local = pl.multiple_of(g * 2 * SUB, 2 * SUB)
        start = pl.multiple_of((first_group + g) * 2 * SUB, 2 * SUB)

        def slab(k):
            return blocks[0, pl.ds(start, 2 * SUB), lanes_of(k)].astype(F32)

        def keep(b, q, tile):
            s_ref[b * RANK + SUB * q : b * RANK + SUB * (q + 1), :] = tile

        unpack_both(lambda k: slab(k)[:SUB], lambda k: slab(k)[SUB:], keep)

        def entry(table, pick, ref, b):
            return table[pl.ds(pl.multiple_of(pick(ref, start + b) * WIDE, WIDE), WIDE), :]

        for b in range(SUB):
            block = s_ref[b * RANK : (b + 1) * RANK, :].astype(BF16)
            rows = jnp.concatenate(
                [entry(left, left_of, left_pick, n)[:, :RANK] for n in (b, b + SUB)], axis=0
            )
            x = dot(rows, block)
            x = beside(x[:RANK], x[WIDE : WIDE + RANK]) + beside(
                x[RANK:WIDE], x[WIDE + RANK :]
            )
            first = entry(left, right_of, right_pick, b)
            second = entry(right, right_of, right_pick, b + SUB)
            weights = jnp.concatenate(
                [first[:RANK], second[:RANK], first[RANK:], second[RANK:]], axis=0
            )
            y = dot(stacked(x), weights, 1)
            y = y[:RANK] + y[RANK:]
            y_ref[b * RANK : (b + 1) * RANK, :] = y[:, :WIDE] + y[:, WIDE:]
        for q in range(NB):
            rows = swap8(
                [y_ref[b * RANK + SUB * q : b * RANK + SUB * (q + 1), :] for b in range(SUB)]
            )
            for k in range(SUB // 2):
                even, odd = rows[2 * k], rows[2 * k + 1]
                at = lanes_of(SUB // 2 * q + k)
                out[pl.ds(local, SUB), at] = beside(even, swapped(odd))
                out[pl.ds(pl.multiple_of(local + SUB, SUB), SUB), at] = beside(
                    swapped(even), odd
                )
        copy(g).start()

    for g in range(groups):
        group(g, s_ref.at[g % 2], y_ref.at[g % 2])
    for g in range(groups):
        copy(g).wait()


def shape(*dims):
    return jax.ShapeDtypeStruct(dims, F32)


def scratch(rows, lanes=WIDE):
    return pltpu.VMEM((rows, lanes), F32)


def call(kernel, outs, specs, scratches=(), limit=8):
    return pl.pallas_call(
        kernel,
        out_shape=outs,
        in_specs=specs,
        out_specs=jax.tree.map(lambda _: VMEM, outs),
        scratch_shapes=list(scratches),
        compiler_params=pltpu.CompilerParams(vmem_limit_bytes=limit << 20),
    )


def partner(value, axis, bit):
    return lax.ppermute(value, axis, [(i, i ^ 1 << bit) for i in range(lax.axis_size(axis))])


def body(
    row_bases,
    col_bases,
    row_transfer,
    col_transfer,
    row_order,
    col_order,
    leaf_pattern,
    leaf_blocks,
    root_rows,
    root_cols,
    root_blocks,
):
    count = row_bases.shape[1]
    nr, nc = lax.axis_size("row"), lax.axis_size("col")
    lr, lc = nr.bit_length() - 1, nc.bit_length() - 1
    top = lr + lc - 1

    leaf_gram, row_pay, col_pay, high, leaf_pattern, root_rows, root_cols = call(
        functools.partial(tree_kernel, count),
        [shape(count * RANK, WIDE), shape(WIDE, WIDE), shape(WIDE, WIDE), shape(RANK, WIDE)]
        + [jax.ShapeDtypeStruct(x.shape, x.dtype) for x in (leaf_pattern, root_rows, root_cols)],
        [HBM] * 9,
        [pltpu.VMEM(x.shape, F32) for x in (row_bases, col_bases, row_transfer, col_transfer)]
        + [pltpu.SMEM(x.shape, jnp.int32) for x in (row_order, col_order)]
        + [scratch(count * RANK), scratch(2 * count * RANK), pltpu.SemaphoreType.DMA((9,))],
    )(
        *(
            pltpu.with_memory_space_constraint(x, pltpu.HBM)
            for x in (
                row_order,
                col_order,
                row_bases,
                col_bases,
                row_transfer,
                col_transfer,
                leaf_pattern,
                root_rows,
                root_cols,
            )
        )
    )

    def step(levels, pay, axis, bit, high, held=0, apart=False, extra=None):
        recv = partner(pay, axis, bit)
        rows = sum(level < top for _, level in levels) * RANK
        rows += 0 if apart else held * RANK
        rows += 0 if extra is None else WIDE
        outs = [shape(RANK, WIDE)]
        if rows:
            outs.append(shape(rows, WIDE))
        if apart:
            outs.append(shape(held * RANK, WIDE))
        args = [pay, recv, high] + ([] if extra is None else [extra])
        result = call(
            functools.partial(step_kernel, levels, top, (nr, nc), held, apart, extra is not None),
            outs,
            [VMEM] * len(args),
            limit=2 + held // 4,
        )(*args)
        return result

    pay = col_pay
    for h in range(lr):
        done = h == lr - 1
        high, pay, *rest = step(
            [("c", h)],
            pay,
            "row",
            h,
            high,
            held=1 << h,
            apart=done,
            extra=row_pay if done else None,
        )
    col_roots = rest[0]
    for h in range(lc):
        done = h == lc - 1
        high, pay, *rest = step(
            [("r", h), ("c", lr + h)], pay, "col", h, high, held=1 << h, apart=done
        )
    row_roots = rest[0]
    for h in range(lr):
        high, *rest = step([("r", lc + h)], pay, "row", h, high)
        pay = rest[0] if rest else None

    big = [pltpu.VMEM((RANK, RANK, WIDE), F32)] * 2 + [pltpu.VMEM((RANK, SUB, WIDE), F32)]

    def leaf_tables(count, gram):
        parts = call(
            chol_first_kernel,
            [
                shape(RANK, RANK, WIDE),
                shape(RANK, RANK, WIDE),
                shape(RANK, SUB, WIDE),
            ],
            [VMEM],
        )(gram)
        out = jax.ShapeDtypeStruct((2 * count * WIDE, WIDE), BF16)
        return call(
            functools.partial(chol_second_kernel, count), [out, out], [VMEM] * 3, big[1:], limit=12
        )(*parts)

    def root_tables(count, *sources):
        factors = call(
            chol_kernel, shape(RANK, RANK, WIDE), [VMEM] * len(sources), big[1:]
        )(*sources)
        out = jax.ShapeDtypeStruct((2 * count * WIDE, WIDE), BF16)
        return call(
            functools.partial(table_kernel, count), [out, out], [VMEM], limit=5 + count // 4
        )(factors)

    def couple(parts, left_of, right_of, left_pick, right_pick, factors, blocks):
        result, first = [], 0
        for groups in parts:
            pairs = groups * 2 * SUB
            result = [
                pl.pallas_call(
                    functools.partial(couple_kernel, first, groups, left_of, right_of),
                    out_shape=shape(1, blocks.shape[1], RANK * RANK),
                    in_specs=[SMEM, SMEM, VMEM, VMEM, VMEM] + [HBM] * len(result),
                    out_specs=HBM,
                    scratch_shapes=[
                        pltpu.VMEM((2, SUB * RANK, WIDE), F32),
                        pltpu.VMEM((2, SUB * RANK, WIDE), F32),
                        scratch(pairs, RANK * RANK),
                        pltpu.SemaphoreType.DMA((groups,)),
                    ],
                    input_output_aliases={5: 0} if result else {},
                    compiler_params=pltpu.CompilerParams(vmem_limit_bytes=6 << 20),
                )(left_pick, right_pick, *factors, blocks, *result)
            ]
            first += groups
        return result[0]

    leaf_groups = leaf_blocks.shape[1] // (2 * SUB)
    root_groups = root_blocks.shape[1] // (2 * SUB)
    leaf_coupled = couple(
        (leaf_groups // 2, leaf_groups - leaf_groups // 2),
        lambda ref, b: ref[0, 0, b],
        lambda ref, b: ref[0, 1, b] + count,
        leaf_pattern,
        leaf_pattern,
        leaf_tables(count, leaf_gram),
        leaf_blocks,
    )
    row_slots, col_slots = nc // 2, nr // 2
    slots = row_slots + col_slots
    root_coupled = couple(
        (root_groups,),
        lambda ref, b: (ref[0, 0, b] & 1) * slots + (ref[0, 0, b] >> 1),
        lambda ref, b: (ref[0, 0, b] & 1) * slots + (ref[0, 0, b] >> 1) + row_slots,
        root_rows,
        root_cols,
        root_tables(slots, row_roots, col_roots),
        root_blocks,
    )
    row_upper_r, col_upper_r = call(
        final_kernel, [shape(1, 1, RANK * RANK), shape(1, 1, RANK * RANK)], [VMEM], big
    )(high)
    return (leaf_coupled, root_coupled, row_upper_r, col_upper_r)


def solution(mesh):
    return jax.shard_map(
        body,
        mesh=mesh,
        in_specs=(
            P("row", "col", None),
            P("col", "row", None),
            P("row", "col", None),
            P("col", "row", None),
            P("row", "col", None),
            P("col", "row", None),
            P("row", "col", None),
            P("row", "col", None),
            P("row", "col", None),
            P("row", "col", None),
            P("row", "col", None),
        ),
        out_specs=(
            P("row", "col", None),
            P("row", "col", None),
            P("row", "col", None),
            P("col", "row", None),
        ),
        check_vma=False,
    )
```

```python
import functools

import jax
import jax.numpy as jnp
from jax import lax
from jax.experimental import pallas as pl
from jax.experimental.pallas import tpu as pltpu
from jax.sharding import PartitionSpec as P


RANK = 64
WIDE = 2 * RANK
SUB = 8
NB = RANK // SUB
F32 = jnp.float32
BF16 = jnp.bfloat16
VMEM = pl.BlockSpec(memory_space=pltpu.VMEM)
SMEM = pl.BlockSpec(memory_space=pltpu.SMEM)
HBM = pl.BlockSpec(memory_space=pltpu.HBM)


def split(x):
    high = x.astype(BF16)
    return high, (x - high.astype(F32)).astype(BF16)


def dot(a, b, rhs_dim=0):
    return lax.dot_general(a, b, (((1,), (rhs_dim,)), ((), ())), preferred_element_type=F32)


def dot3(a, b):
    a_high, a_low = split(a)
    b_high, b_low = split(b)
    return dot(a_high, b_high) + (dot(a_high, b_low) + dot(a_low, b_high))


def stacked(x, axis=0):
    return jnp.concatenate(split(x), axis=axis)


def lane_half(rows):
    return lax.broadcasted_iota(jnp.int32, (rows, WIDE), 1) < RANK


def swapped(x):
    return pltpu.roll(x, RANK, 1)


def beside(left, right):
    return jnp.where(lane_half(left.shape[0]), left, right)


def dot_both(a, b):
    y = dot(stacked(a), stacked(b))
    return beside(y[:RANK], y[RANK:WIDE]) + beside(y[WIDE : WIDE + RANK], y[WIDE + RANK :])


def sandwich_both(gram, transfer):
    x = dot(stacked(jnp.concatenate([transfer, transfer], axis=0).T), stacked(gram))
    x = x[:WIDE] + x[WIDE:]
    top, low = x[:RANK], x[RANK:]
    return dot_both(
        jnp.concatenate([beside(top, swapped(top)), beside(swapped(low), low)], axis=0), transfer
    )


def swap8(tiles):
    tiles = list(tiles)
    sub = lax.broadcasted_iota(jnp.int32, tiles[0].shape, 0)
    for d in (4, 2, 1):
        keep = (sub & d) == 0
        for i in range(SUB):
            if not i & d:
                a, b = tiles[i], tiles[i + d]
                tiles[i] = jnp.where(keep, a, pltpu.roll(b, d, 0))
                tiles[i + d] = jnp.where(keep, pltpu.roll(a, SUB - d, 0), b)
    return tiles


def eight(n):
    return slice(SUB * n, SUB * (n + 1))


def unpack_both(left, right, store):
    for q in range(NB):
        rows = []
        for k in range(SUB // 2 * q, SUB // 2 * (q + 1)):
            a, b = left(k), right(k)
            rows += [beside(a, swapped(b)), beside(swapped(a), b)]
        for b, tile in enumerate(swap8(rows)):
            store(b, q, tile)


def lanes_of(k):
    return slice(k * WIDE, (k + 1) * WIDE)


def unpack_trees(left_ref, right_ref, out_ref, count):
    for g in range(count // SUB):

        def store(b, q, tile):
            at = (SUB * g + b) * RANK + SUB * q
            out_ref[at : at + SUB, :] = tile

        unpack_both(
            lambda k: left_ref[0, eight(g), lanes_of(k)],
            lambda k: right_ref[0, eight(g), lanes_of(k)],
            store,
        )


def tree_kernel(
    count,
    row_order_in,
    col_order_in,
    row_bases_in,
    col_bases_in,
    row_transfer_in,
    col_transfer_in,
    *refs,
):
    picks_in, refs = refs[:3], refs[3:]
    leaf_gram, row_pay, col_pay, high = refs[:4]
    picks, refs = refs[4:7], refs[7:]
    (
        row_bases,
        col_bases,
        row_transfer,
        col_transfer,
        row_order,
        col_order,
        basis,
        trans,
        sems,
    ) = refs
    copies = [
        pltpu.make_async_copy(source, target, sems.at[n])
        for n, (source, target) in enumerate(
            (
                (row_bases_in, row_bases),
                (col_bases_in, col_bases),
                (row_transfer_in, row_transfer),
                (col_transfer_in, col_transfer),
                (row_order_in, row_order),
                (col_order_in, col_order),
                *zip(picks_in, picks),
            )
        )
    ]
    for copy in copies:
        copy.start()
    copies[0].wait()
    copies[1].wait()
    unpack_trees(row_bases, col_bases, basis, count)
    for leaf in range(count):
        u = basis[leaf * RANK : (leaf + 1) * RANK, :]
        leaf_gram[leaf * RANK : (leaf + 1) * RANK, :] = dot_both(
            jnp.concatenate([u, u], axis=0).T, u
        )
    for copy in copies[2:6]:
        copy.wait()
    unpack_trees(row_transfer, col_transfer, trans, 2 * count)
    nodes = []
    for q in range(count // 2):
        total = None
        for p in (2 * q, 2 * q + 1):
            r = pl.ds(pl.multiple_of(row_order[0, 0, p] * RANK, RANK), RANK)
            c = pl.ds(pl.multiple_of(col_order[0, 0, p] * RANK, RANK), RANK)
            term = sandwich_both(
                beside(leaf_gram[r, :], leaf_gram[c, :]), beside(trans[r, :], trans[c, :])
            )
            total = term if total is None else total + term
        nodes.append(total)
    offset = count
    while len(nodes) > 1:
        terms = []
        for q, gram in enumerate(nodes):
            terms.append(
                sandwich_both(gram, trans[(offset + q) * RANK : (offset + q + 1) * RANK, :])
            )
        offset += len(nodes)
        nodes = [terms[2 * q] + terms[2 * q + 1] for q in range(len(terms) // 2)]
    gram = nodes[0]
    term = sandwich_both(gram, trans[offset * RANK : (offset + 1) * RANK, :])
    first = trans[(offset + 1) * RANK : (offset + 2) * RANK, :]
    high[...] = gram
    row_pay[0:RANK, :] = beside(term, swapped(first))
    row_pay[RANK:WIDE, :] = gram
    col_pay[0:RANK, :] = beside(swapped(term), first)
    col_pay[RANK:WIDE, :] = swapped(gram)
    for copy in copies[6:]:
        copy.wait()


def step_kernel(levels, top, sizes, held, apart, extra, own, recv, high_in, *refs):
    refs = list(refs)
    before = refs.pop(0) if extra else None
    high_out = refs.pop(0)
    roots_out = refs.pop() if apart else None
    pay_out = refs.pop(0) if refs else None
    nr, nc = sizes
    i, j = lax.axis_index("row"), lax.axis_index("col")
    base = 0
    if extra:
        pay_out[0:RANK, :] = before[0:RANK, :]
        base = RANK
    high = high_in[...]
    uppers = []
    for slot, (name, level) in enumerate(levels):
        d = i * nc + j if name == "r" else j * nr + i
        span = 1 << level
        upper = lax.rem(lax.div(d, span), 2) == 1
        uppers.append(upper)
        take = lax.rem(d, 2 * span) == span
        if level == top:
            take = jnp.logical_or(take, d == 0)
        mine = own[slot * RANK : (slot + 1) * RANK, :]
        theirs = recv[slot * RANK : (slot + 1) * RANK, :]
        total = mine + theirs
        if level < top:
            transfer = jnp.where(upper, mine, theirs)
            first = jnp.where(upper, theirs, mine)
            x = dot3(transfer.T[RANK:], total[:, :RANK])
            pay_out[base : base + RANK, :] = beside(swapped(dot3(x, transfer)), first)
            base += RANK
        picked = beside(total, high) if name == "r" else beside(high, swapped(total))
        high = jnp.where(take, picked, high)
    high_out[...] = high
    if extra:
        pay_out[base : base + RANK, :] = before[RANK:WIDE, :]
    if held:
        upper = uppers[0]
        start = len(levels) * RANK
        if roots_out is None:
            roots_out = pay_out.at[base:, :]
        if held == 1:
            mine = own[start : start + RANK, :]
            theirs = recv[start : start + RANK, :]
            roots_out[0:RANK, :] = jnp.where(
                upper, beside(theirs, swapped(mine)), beside(mine, swapped(theirs))
            )
        else:
            rows = held // 2 * RANK
            mine = own[start : start + rows, :]
            theirs = recv[start : start + rows, :]
            roots_out[0:rows, :] = jnp.where(upper, theirs, mine)
            roots_out[rows : 2 * rows, :] = jnp.where(upper, mine, theirs)


def chol_lanes(a_ref, r_ref, scale_ref, begin=-1, end=NB - 1):
    sub = lax.broadcasted_iota(jnp.int32, (SUB, WIDE), 0)
    here = lax.axis_index("row") >= 0

    def spread(i, j):
        return r_ref[i, pl.ds(j, SUB, stride=0), :]

    def less(value, f, row):
        return lax.sub(value, lax.mul(f, row))

    def reduced(p, qs):
        acc = {(r, q): a_ref[SUB * p + r, eight(q), :] for r in range(SUB) for q in qs}
        for k in range(SUB * p):
            rows = [r_ref[k, eight(q), :] for q in qs]
            for r in range(SUB):
                f = spread(k, SUB * p + r)
                for q, row in zip(qs, rows):
                    acc[r, q] = less(acc[r, q], f, row)
        return acc

    def diagonal(p):
        acc = reduced(p, [p])
        for r in range(SUB):
            inv = lax.rsqrt(jnp.broadcast_to(acc[r, p][r : r + 1, :], (SUB, WIDE)))
            scale_ref[SUB * p + r] = inv
            row = jnp.where(sub >= r, lax.mul(acc[r, p], inv), 0.0)
            r_ref[SUB * p + r, eight(p), :] = row
            for r2 in range(r + 1, SUB):
                f = jnp.broadcast_to(row[r2 : r2 + 1, :], (SUB, WIDE))
                acc[r2, p] = less(acc[r2, p], f, row)

    def beyond(p, qs):
        acc = reduced(p, qs)
        for r in range(SUB):
            inv = scale_ref[SUB * p + r]
            for q in qs:
                acc[r, q] = lax.mul(acc[r, q], inv)
                r_ref[SUB * p + r, eight(q), :] = acc[r, q]
            for r2 in range(r + 1, SUB):
                f = spread(SUB * p + r, SUB * p + r2)
                for q in qs:
                    acc[r2, q] = less(acc[r2, q], f, acc[r, q])

    for p in range(begin, end):

        @pl.when(here)
        def _():
            if p >= 0:
                beyond(p, [p + 1])
            diagonal(p + 1)
            for q in range(p + 2, NB, 2):
                if p >= 0:
                    beyond(p, list(range(q, min(q + 2, NB))))


CELL = WIDE // SUB
CUT = NB // 2


def load_slots(slots, a_ref):
    cell = lax.broadcasted_iota(jnp.int32, (RANK, WIDE), 1) % SUB
    for q in range(NB):
        b0 = SUB * q
        if len(slots) <= SUB:
            group = slots + [slots[-1]] * (SUB - len(slots))
            tiles = [ref[s * RANK + b0 : s * RANK + b0 + SUB, :] for ref, s in group]
            t = jnp.concatenate(tiles, axis=0).T
            value = jnp.concatenate([t[b0:RANK], t[RANK + b0 :]], axis=1)
            for r in range(SUB):
                a_ref[b0 + r, b0:RANK, :] = pltpu.roll(value, WIDE - r, 1) if r else value
            continue
        turned = []
        for g in range(0, len(slots), CELL):
            group = slots[g : g + CELL]
            group = group + [group[-1]] * (CELL - len(group))
            tiles = [ref[s * RANK + b0 : s * RANK + b0 + SUB, :] for ref, s in group]
            t = jnp.concatenate(tiles, axis=0).T
            turned += [t[b0:RANK], t[RANK + b0 :]]
        for r in range(SUB):
            value = None
            for offset, t in enumerate(turned):
                t = pltpu.roll(t, (offset - r) % WIDE, 1) if offset != r else t
                value = t if value is None else jnp.where(cell[b0:] == offset, t, value)
            a_ref[b0 + r, b0:RANK, :] = value


def factor_tiles(r_ref, q, group):
    cell = lax.broadcasted_iota(jnp.int32, (SUB, WIDE), 1) % SUB
    columns = []
    for half in range(2):
        offset = 0 if group is None else 2 * group + half
        if group is None and half:
            columns += columns
            break
        for p in range(NB):
            tile = jnp.zeros((SUB, WIDE), F32)
            for r in range(SUB if p >= q else 0):
                v = r_ref[SUB * q + r, eight(p), :]
                v = pltpu.roll(v, (r - offset) % WIDE, 1) if offset != r else v
                tile = jnp.where(cell == r, v, tile)
            columns.append(tile)
    return jnp.concatenate(columns, axis=0).T


def chol_kernel(*refs):
    *inputs, r_ref, a_ref, scale_ref = refs
    slots = [(ref, s) for ref in inputs for s in range(ref.shape[0] // RANK)]
    load_slots(slots, a_ref)
    chol_lanes(a_ref, r_ref, scale_ref)


def chol_first_kernel(gram, r_ref, a_ref, scale_ref):
    slots = [(gram, s) for s in range(gram.shape[0] // RANK)]
    load_slots(slots, a_ref)
    chol_lanes(a_ref, r_ref, scale_ref, -1, CUT)


def chol_second_kernel(count, r_in, a_ref, scale_in, left, right, r_ref, scale_ref):
    for k in range(SUB * (CUT + 1)):
        last = CUT + 1 if k >= SUB * CUT else NB
        at = slice(SUB * (k // SUB), SUB * last)
        r_ref[k, at, :] = r_in[k, at, :]
    for k in range(SUB * CUT, SUB * (CUT + 1)):
        scale_ref[k] = scale_in[k]
    chol_lanes(a_ref, r_ref, scale_ref, CUT, NB - 1)
    table_kernel(count, r_ref, left, right)


def table_kernel(count, r_ref, left, right):
    keep = lane_half(2 * SUB)
    for q in range(0, NB, 2):
        if count <= SUB:
            upper = factor_tiles(r_ref, q, None)
            lower = factor_tiles(r_ref, q + 1, None)
            for half in range(2):
                for s in range(count):
                    rows = eight(SUB * half + s)
                    both = jnp.concatenate([upper[rows], lower[rows]], axis=0)
                    at = (half * count + s) * WIDE + SUB * q
                    for table, value in (
                        (left, jnp.where(keep, both, 0.0)),
                        (right, jnp.where(keep, 0.0, both)),
                    ):
                        high, low = split(value)
                        table[at : at + 2 * SUB, :] = high
                        table[at + RANK : at + RANK + 2 * SUB, :] = low
            continue
        for g in range(-(-count // CELL)):
            upper = factor_tiles(r_ref, q, g)
            lower = factor_tiles(r_ref, q + 1, g)
            for b in range(min(CELL, count - CELL * g)):
                both = jnp.concatenate([upper[eight(b)], lower[eight(b)]], axis=0)
                other = swapped(both)
                s = CELL * g + b
                for n, here, there in ((s, both, other), (count + s, other, both)):
                    at = n * WIDE + SUB * q
                    for table, value in (
                        (left, jnp.where(keep, here, 0.0)),
                        (right, jnp.where(keep, 0.0, there)),
                    ):
                        high, low = split(value)
                        table[at : at + 2 * SUB, :] = high
                        table[at + RANK : at + RANK + 2 * SUB, :] = low


def final_kernel(high, row_out, col_out, a_ref, r_ref, scale_ref):
    for i in range(RANK):
        b0 = SUB * (i // SUB)
        value = high[b0:RANK, :]
        a_ref[i, b0:RANK, :] = pltpu.roll(value, WIDE - i, 1) if i else value
    chol_lanes(a_ref, r_ref, scale_ref)
    lane = lax.broadcasted_iota(jnp.int32, (SUB, WIDE), 1) % RANK
    columns = []
    for q in range(NB):
        tile = jnp.zeros((SUB, WIDE), F32)
        for i in range(SUB * (q + 1)):
            value = r_ref[i, eight(q), :]
            tile = jnp.where(lane == i, pltpu.roll(value, i, 1) if i else value, tile)
        columns.append(tile)
    columns = jnp.concatenate(columns, axis=0)
    rows = jnp.concatenate([columns, columns], axis=0).T
    for out, half in ((row_out, rows[:RANK]), (col_out, rows[RANK:])):
        for k in range(RANK // 2):
            out[0, 0:1, lanes_of(k)] = beside(half[2 * k : 2 * k + 1], half[2 * k + 1 : 2 * k + 2])


def unpack_blocks(blocks, start, s_ref):
    def slab(k):
        return blocks[0, pl.ds(start, 2 * SUB), lanes_of(k)].astype(F32)

    def keep(b, q, tile):
        s_ref[b * RANK + SUB * q : b * RANK + SUB * (q + 1), :] = tile

    unpack_both(lambda k: slab(k)[:SUB], lambda k: slab(k)[SUB:], keep)


def unpack_kernel(groups, blocks, out, s_ref):
    for g in range(groups):
        unpack_blocks(blocks, g * 2 * SUB, s_ref.at[g % 2])
        out[g * SUB * RANK : (g + 1) * SUB * RANK, :] = s_ref[g % 2].astype(BF16)


def couple_kernel(
    first_group, groups, left_of, right_of, left_pick, right_pick, left, right, blocks, *refs
):
    target, s_ref, y_ref, out, sem = refs[-5:]

    def copy(g):
        at = pl.ds(pl.multiple_of(g * 2 * SUB, 2 * SUB), 2 * SUB)
        to = pl.ds(pl.multiple_of((first_group + g) * 2 * SUB, 2 * SUB), 2 * SUB)
        return pltpu.make_async_copy(out.at[at, :], target.at[0, to, :], sem.at[g])

    def group(g, s_ref, y_ref):
        local = pl.multiple_of(g * 2 * SUB, 2 * SUB)
        start = pl.multiple_of((first_group + g) * 2 * SUB, 2 * SUB)

        if blocks.ndim == 3:
            unpack_blocks(blocks, start, s_ref)

        def entry(table, pick, ref, b):
            return table[pl.ds(pl.multiple_of(pick(ref, start + b) * WIDE, WIDE), WIDE), :]

        for b in range(SUB):
            if blocks.ndim == 3:
                block = s_ref[b * RANK : (b + 1) * RANK, :].astype(BF16)
            else:
                at = ((first_group + g) * SUB + b) * RANK
                block = blocks[at : at + RANK, :]
            rows = jnp.concatenate(
                [entry(left, left_of, left_pick, n)[:, :RANK] for n in (b, b + SUB)], axis=0
            )
            x = dot(rows, block)
            x = beside(x[:RANK], x[WIDE : WIDE + RANK]) + beside(
                x[RANK:WIDE], x[WIDE + RANK :]
            )
            first = entry(left, right_of, right_pick, b)
            second = entry(right, right_of, right_pick, b + SUB)
            weights = jnp.concatenate(
                [first[:RANK], second[:RANK], first[RANK:], second[RANK:]], axis=0
            )
            y = dot(stacked(x), weights, 1)
            y = y[:RANK] + y[RANK:]
            y_ref[b * RANK : (b + 1) * RANK, :] = y[:, :WIDE] + y[:, WIDE:]
        for q in range(NB):
            rows = swap8(
                [y_ref[b * RANK + SUB * q : b * RANK + SUB * (q + 1), :] for b in range(SUB)]
            )
            for k in range(SUB // 2):
                even, odd = rows[2 * k], rows[2 * k + 1]
                at = lanes_of(SUB // 2 * q + k)
                out[pl.ds(local, SUB), at] = beside(even, swapped(odd))
                out[pl.ds(pl.multiple_of(local + SUB, SUB), SUB), at] = beside(
                    swapped(even), odd
                )
        copy(g).start()

    for g in range(groups):
        group(g, s_ref.at[g % 2], y_ref.at[g % 2])
    for g in range(groups):
        copy(g).wait()


def shape(*dims):
    return jax.ShapeDtypeStruct(dims, F32)


def scratch(rows, lanes=WIDE):
    return pltpu.VMEM((rows, lanes), F32)


def call(kernel, outs, specs, scratches=(), limit=8):
    return pl.pallas_call(
        kernel,
        out_shape=outs,
        in_specs=specs,
        out_specs=jax.tree.map(lambda _: VMEM, outs),
        scratch_shapes=list(scratches),
        compiler_params=pltpu.CompilerParams(vmem_limit_bytes=limit << 20),
    )


def partner(value, axis, bit):
    return lax.ppermute(value, axis, [(i, i ^ 1 << bit) for i in range(lax.axis_size(axis))])


def body(
    row_bases,
    col_bases,
    row_transfer,
    col_transfer,
    row_order,
    col_order,
    leaf_pattern,
    leaf_blocks,
    root_rows,
    root_cols,
    root_blocks,
):
    count = row_bases.shape[1]
    nr, nc = lax.axis_size("row"), lax.axis_size("col")
    lr, lc = nr.bit_length() - 1, nc.bit_length() - 1
    top = lr + lc - 1

    leaf_gram, row_pay, col_pay, high, leaf_pattern, root_rows, root_cols = call(
        functools.partial(tree_kernel, count),
        [shape(count * RANK, WIDE), shape(WIDE, WIDE), shape(WIDE, WIDE), shape(RANK, WIDE)]
        + [jax.ShapeDtypeStruct(x.shape, x.dtype) for x in (leaf_pattern, root_rows, root_cols)],
        [HBM] * 9,
        [pltpu.VMEM(x.shape, F32) for x in (row_bases, col_bases, row_transfer, col_transfer)]
        + [pltpu.SMEM(x.shape, jnp.int32) for x in (row_order, col_order)]
        + [scratch(count * RANK), scratch(2 * count * RANK), pltpu.SemaphoreType.DMA((9,))],
    )(
        *(
            pltpu.with_memory_space_constraint(x, pltpu.HBM)
            for x in (
                row_order,
                col_order,
                row_bases,
                col_bases,
                row_transfer,
                col_transfer,
                leaf_pattern,
                root_rows,
                root_cols,
            )
        )
    )

    def step(levels, pay, axis, bit, high, held=0, apart=False, extra=None):
        recv = partner(pay, axis, bit)
        rows = sum(level < top for _, level in levels) * RANK
        rows += 0 if apart else held * RANK
        rows += 0 if extra is None else WIDE
        outs = [shape(RANK, WIDE)]
        if rows:
            outs.append(shape(rows, WIDE))
        if apart:
            outs.append(shape(held * RANK, WIDE))
        args = [pay, recv, high] + ([] if extra is None else [extra])
        result = call(
            functools.partial(step_kernel, levels, top, (nr, nc), held, apart, extra is not None),
            outs,
            [VMEM] * len(args),
            limit=2 + held // 4,
        )(*args)
        return result

    pay = col_pay
    for h in range(lr):
        done = h == lr - 1
        high, pay, *rest = step(
            [("c", h)],
            pay,
            "row",
            h,
            high,
            held=1 << h,
            apart=done,
            extra=row_pay if done else None,
        )
    col_roots = rest[0]
    for h in range(lc):
        done = h == lc - 1
        high, pay, *rest = step(
            [("r", h), ("c", lr + h)], pay, "col", h, high, held=1 << h, apart=done
        )
    row_roots = rest[0]
    for h in range(lr):
        high, *rest = step([("r", lc + h)], pay, "row", h, high)
        pay = rest[0] if rest else None

    big = [pltpu.VMEM((RANK, RANK, WIDE), F32)] * 2 + [pltpu.VMEM((RANK, SUB, WIDE), F32)]

    def leaf_tables(count, gram):
        parts = call(
            chol_first_kernel,
            [
                shape(RANK, RANK, WIDE),
                shape(RANK, RANK, WIDE),
                shape(RANK, SUB, WIDE),
            ],
            [VMEM],
        )(gram)
        out = jax.ShapeDtypeStruct((2 * count * WIDE, WIDE), BF16)
        return call(
            functools.partial(chol_second_kernel, count), [out, out], [VMEM] * 3, big[1:], limit=12
        )(*parts)

    def root_tables(count, *sources):
        factors = call(
            chol_kernel, shape(RANK, RANK, WIDE), [VMEM] * len(sources), big[1:]
        )(*sources)
        out = jax.ShapeDtypeStruct((2 * count * WIDE, WIDE), BF16)
        return call(
            functools.partial(table_kernel, count), [out, out], [VMEM], limit=5 + count // 4
        )(factors)

    def couple(parts, left_of, right_of, left_pick, right_pick, factors, blocks):
        result, first = [], 0
        for groups in parts:
            pairs = groups * 2 * SUB
            result = [
                pl.pallas_call(
                    functools.partial(couple_kernel, first, groups, left_of, right_of),
                    out_shape=shape(1, sum(parts) * 2 * SUB, RANK * RANK),
                    in_specs=[SMEM, SMEM, VMEM, VMEM, VMEM] + [HBM] * len(result),
                    out_specs=HBM,
                    scratch_shapes=[
                        pltpu.VMEM((2, SUB * RANK, WIDE), F32),
                        pltpu.VMEM((2, SUB * RANK, WIDE), F32),
                        scratch(pairs, RANK * RANK),
                        pltpu.SemaphoreType.DMA((groups,)),
                    ],
                    input_output_aliases={5: 0} if result else {},
                    compiler_params=pltpu.CompilerParams(vmem_limit_bytes=6 << 20),
                )(left_pick, right_pick, *factors, blocks, *result)
            ]
            first += groups
        return result[0]

    leaf_groups = leaf_blocks.shape[1] // (2 * SUB)
    root_groups = root_blocks.shape[1] // (2 * SUB)
    leaf_coupled = couple(
        (leaf_groups // 2, leaf_groups - leaf_groups // 2),
        lambda ref, b: ref[0, 0, b],
        lambda ref, b: ref[0, 1, b] + count,
        leaf_pattern,
        leaf_pattern,
        leaf_tables(count, leaf_gram),
        leaf_blocks,
    )
    row_slots, col_slots = nc // 2, nr // 2
    slots = row_slots + col_slots
    root_squares = call(
        functools.partial(unpack_kernel, root_groups),
        jax.ShapeDtypeStruct((root_groups * SUB * RANK, WIDE), BF16),
        [VMEM],
        [pltpu.VMEM((2, SUB * RANK, WIDE), F32)],
        limit=4,
    )(root_blocks)
    root_coupled = couple(
        (root_groups,),
        lambda ref, b: (ref[0, 0, b] & 1) * slots + (ref[0, 0, b] >> 1),
        lambda ref, b: (ref[0, 0, b] & 1) * slots + (ref[0, 0, b] >> 1) + row_slots,
        root_rows,
        root_cols,
        root_tables(slots, row_roots, col_roots),
        root_squares,
    )
    row_upper_r, col_upper_r = call(
        final_kernel, [shape(1, 1, RANK * RANK), shape(1, 1, RANK * RANK)], [VMEM], big
    )(high)
    return (leaf_coupled, root_coupled, row_upper_r, col_upper_r)


def solution(mesh):
    return jax.shard_map(
        body,
        mesh=mesh,
        in_specs=(
            P("row", "col", None),
            P("col", "row", None),
            P("row", "col", None),
            P("col", "row", None),
            P("row", "col", None),
            P("col", "row", None),
            P("row", "col", None),
            P("row", "col", None),
            P("row", "col", None),
            P("row", "col", None),
            P("row", "col", None),
        ),
        out_specs=(
            P("row", "col", None),
            P("row", "col", None),
            P("row", "col", None),
            P("col", "row", None),
        ),
        check_vma=False,
    )
```
